32 devices in a mesh: group: 2 (over y), lon: 4 (over z), lat: 2 (over x), fld: 2 (over core).
Axes of the slice: x: 2, y: 2, z: 4, core: 2. Of those that a mesh axis runs over, the one named last changes fastest.
Arguments:
- background: float32 [8, 32, 8192], P('group', ('lat', 'fld'), 'lon'), parts along dimension 0, may hold values from -7.2 to 7.2
- decay_sq: float32 [4, 32, 8192], P(None, ('lat', 'fld'), 'lon'), may hold values from 0.02 to 0.5
- edge_weight: float32 [4, 32, 8192], P(None, ('lat', 'fld'), 'lon'), may hold values from 0.1 to 1
- coupling: float32 [4, 4], replicated, may hold values from -0.32 to 1.6, as said below
- obs_tiles: bfloat16 [256, 256, 256], P(('lon', 'lat', 'fld')), may hold values from -0.375 to 0.375
- obs_values: float32 [512, 256], P(('group', 'lon', 'lat', 'fld')), parts along dimension 0, may hold values from -15 to 15
- obs_weights: float32 [256, 256], P(('lon', 'lat', 'fld')), may hold values from 4 to 32
- obs_counts: int32 [256], P(('lon', 'lat', 'fld')), may hold values from 32 to 256, as said below
- swath_ids: int32 [256], P(('lon', 'lat', 'fld')), may hold values from 0 to 7
- swath_scale: float32 [8], replicated, may hold values from 0.5 to 2
- tile_owner: int32 [256], P(('lon', 'lat', 'fld')), may hold values from 0 to 3, as said below
- tile_slot: int32 [256], P(('lon', 'lat', 'fld')), may hold values from 0 to 255
Outputs:
- solution: float32 [8, 32, 8192], P('group', ('lat', 'fld'), 'lon'), parts along dimension 0
- residual: float32 [8, 32, 8192], P('group', ('lat', 'fld'), 'lon'), parts along dimension 0
The draws below stay inside these ranges and needn't reach their ends.
There are 2 independent parts, one for each index of `group`. The reference program is written for one: setup_inputs(seed, part) draws one part's arguments, and reference() takes and returns one part's arrays. A program takes and returns all parts, laid end to end along the dimension named above; an argument that names none is the same for every part. Nothing has to cross between parts.
Inputs may be any that keep to these rules, and one draw needn't show every extreme that they name: `obs_counts`: each device's 16 tiles include one with all 256 observations live. `tile_owner`: of one device's 16 tiles at most 4 read patches in any one longitude block, and in every block row some longitude block is read by exactly 4 tiles of each device of that block row. `coupling`: Symmetric, each diagonal entry above the sum of the magnitudes of its row's others.
All inputs are finite; a program needn't handle non-finite values.
Results may differ from the reference program's by a relative error of at most 0.0065.
Values may be sent and summed in bfloat16 or wider, within the bound.
A program may use at most 64 MiB of HBM per device.

```python
import math
import jax
import jax.numpy as jnp
from jax import lax

F = 4
DIRS = 4
PATCH = 256
OBS = 256
CAP = 4
SWATHS = 8
ITERS = 3
CLAT = 8
CLON = 2048
TILE_DEV = 16
LON_DEVS = 4
ROW_DEVS = 4
NLAT = 32
NLON = 8192
TILES = 256
NPATCH_DEV = 256


def draw_background(key, part):
    key_rows, key_values = jax.random.split(jax.random.fold_in(key, 5))
    lon_pos = jnp.arange(NLON).astype(jnp.float32)
    ramp = 1.0 + 2.0 * lon_pos / NLON
    row_scale = jnp.exp(jax.random.uniform(key_rows, (NLAT,), jnp.float32, 0.0, math.log(10.0)))
    values = jax.random.truncated_normal(key_values, -4.0, 4.0, (F, NLAT, NLON), jnp.float32)
    return 0.06 * row_scale[None, :, None] * values * ramp[None, None, :]


def draw_coupling(key, part):
    key_off, key_diagonal = jax.random.split(jax.random.fold_in(key, 7))
    drawn = jax.random.uniform(key_off, (F, F), jnp.float32, -0.32, 0.32)
    symmetric = 0.5 * (drawn + drawn.T)
    diagonal = jax.random.uniform(key_diagonal, (F,), jnp.float32, 1.0, 1.6)
    identity = jnp.eye(F, dtype=jnp.float32)
    return symmetric * (1.0 - identity) + identity * diagonal[None, :]


def draw_obs_counts(key, part):
    key_counts, key_full = jax.random.split(jax.random.fold_in(key, 11))
    counts = jax.random.randint(key_counts, (TILES,), OBS // 8, OBS + 1)
    blocks = TILES // TILE_DEV
    chosen = jax.random.randint(key_full, (blocks,), 0, TILE_DEV)
    within = jnp.arange(TILES) % TILE_DEV
    owner_block = jnp.arange(TILES) // TILE_DEV
    return jnp.where(within == chosen[owner_block], OBS, counts).astype(jnp.int32)


def draw_tile_owner(key, part):
    key_hot, key_pool, key_shuffle = jax.random.split(jax.random.fold_in(key, 23), 3)
    blocks = TILES // TILE_DEV
    hottest = jax.random.randint(key_hot, (ROW_DEVS,), 0, LON_DEVS)
    block_hot = hottest[jnp.arange(blocks) % ROW_DEVS]
    pool_size = (LON_DEVS - 1) * CAP
    pool_keys = jax.random.split(key_pool, blocks)
    picked = jax.vmap(lambda member_key: jax.random.permutation(member_key, pool_size))(pool_keys)[:, :TILE_DEV - CAP]
    others = (block_hot[:, None] + 1 + picked // CAP) % LON_DEVS
    assigned = jnp.concatenate([jnp.broadcast_to(block_hot[:, None], (blocks, CAP)), others], axis=1)
    shuffle_keys = jax.random.split(key_shuffle, blocks)
    shuffle = jax.vmap(lambda member_key: jax.random.permutation(member_key, TILE_DEV))(shuffle_keys)
    return jnp.take_along_axis(assigned, shuffle, axis=1).reshape(-1).astype(jnp.int32)


def with_ends(result, key, low, largest):
    spot = [jax.random.randint(jax.random.fold_in(key, axis), (), 0, length) for axis, length in enumerate(result.shape)]
    widest = result.shape.index(max(result.shape))
    beside = spot[:widest] + [(spot[widest] + 1) % result.shape[widest]] + spot[widest + 1:]
    return result.at[tuple(spot)].set(low).at[tuple(beside)].set(largest)


def steps_of(key, shape, cuts, low, top_value):
    level = 1.0
    for dim, blocks in cuts:
        steps = jax.random.uniform(jax.random.fold_in(jax.random.fold_in(key, 6), dim), (blocks,), jnp.float32, low / len(cuts), top_value / len(cuts))
        level = level * jnp.repeat(jnp.exp(steps), shape[dim] // blocks).reshape((-1,) + (1,) * (len(shape) - 1 - dim))
    return level


def bell_draw(own_key, dims, width, most, cuts=(), kind=jnp.bfloat16):
    result = width * jax.random.normal(own_key, dims, jnp.float32)
    if cuts:
        result = result * steps_of(own_key, dims, cuts, -0.22, 0.18)
    return jnp.clip(result, -most, most).astype(kind)


def setup_inputs(seed: int = 0, part: int = 0) -> dict:
    streams_of = jax.random.split(jax.random.key(seed), 13)
    own_keys = jax.random.split(jax.random.fold_in(streams_of[12], part), 13)
    background = draw_background(jax.random.fold_in(jax.random.fold_in(streams_of[12], part), 71), part)
    decay_sq = jnp.clip(jnp.exp(math.log(0.5) - 3.218876 * jax.random.uniform(streams_of[1], (F, NLAT, NLON), jnp.float32) ** steps_of(streams_of[1], (F, NLAT, NLON), ((1, 4), (2, 4)), -0.2, 0.2)), 0.02, 0.5)
    edge_weight = jnp.clip(jnp.exp(math.log(1.0) - 2.3025851 * jax.random.uniform(streams_of[2], (DIRS, NLAT, NLON), jnp.float32) ** steps_of(streams_of[2], (DIRS, NLAT, NLON), ((1, 4), (2, 4)), -0.2, 0.2)), 0.1, 1.0)
    coupling = draw_coupling(jax.random.fold_in(streams_of[12], 71), part)
    obs_tiles = bell_draw(streams_of[4], (TILES, OBS, PATCH), PATCH ** -0.5, 0.375, ((0, 16),))
    obs_values = bell_draw(own_keys[5], (TILES, OBS), 3.0, 15.0, ((0, 16),), jnp.float32)
    obs_weights = jnp.clip(jnp.exp(math.log(32.0) - 2.0794415 * jax.random.uniform(streams_of[6], (TILES, OBS), jnp.float32) ** steps_of(streams_of[6], (TILES, OBS), ((0, 16),), -0.2, 0.2)), 4.0, 32.0)
    obs_counts = draw_obs_counts(jax.random.fold_in(streams_of[12], 71), part)
    swath_ids = with_ends(jax.random.randint(streams_of[8], (TILES,), 0, SWATHS), jax.random.fold_in(streams_of[8], 1), 0, SWATHS - 1).astype(jnp.int32)
    swath_scale = jnp.clip(jnp.exp(jax.random.uniform(streams_of[9], (SWATHS,), jnp.float32, math.log(0.5), math.log(2.0))), 0.5, 2.0)
    tile_owner = draw_tile_owner(jax.random.fold_in(streams_of[12], 71), part)
    tile_slot = with_ends(jax.random.randint(streams_of[11], (TILES,), 0, NPATCH_DEV), jax.random.fold_in(streams_of[11], 1), 0, NPATCH_DEV - 1).astype(jnp.int32)
    return {"background": background, "decay_sq": decay_sq, "edge_weight": edge_weight, "coupling": coupling, "obs_tiles": obs_tiles, "obs_values": obs_values, "obs_weights": obs_weights, "obs_counts": obs_counts, "swath_ids": swath_ids, "swath_scale": swath_scale, "tile_owner": tile_owner, "tile_slot": tile_slot}


DIRECTIONS = ((0, 1), (1, 0), (1, 1), (1, -1))


def stencil(padded, weights_pad, decay_part):
    rows_out = decay_part.shape[-2]
    cols_out = decay_part.shape[-1]

    def window_at(source, step_lat, step_lon):
        return source[..., 1 + step_lat:1 + step_lat + rows_out, 1 + step_lon:1 + step_lon + cols_out]

    center = window_at(padded, 0, 0)
    summed = decay_part * center
    for index_dir in range(4):
        step_lat, step_lon = DIRECTIONS[index_dir]
        weight_here = window_at(weights_pad[index_dir], 0, 0)
        weight_ahead = 0.5 * (weight_here + window_at(weights_pad[index_dir], step_lat, step_lon))
        weight_behind = 0.5 * (weight_here + window_at(weights_pad[index_dir], -step_lat, -step_lon))
        summed = summed + weight_ahead * (center - window_at(padded, step_lat, step_lon))
        summed = summed + weight_behind * (center - window_at(padded, -step_lat, -step_lon))
    return summed


def mix_fields(coupling, field_in):
    return jnp.einsum("fg,gyx->fyx", coupling, field_in, precision=lax.Precision.HIGHEST)


def pad_grid(field_in, pad_depth):
    wrapped = jnp.concatenate([field_in[..., -pad_depth:], field_in, field_in[..., :pad_depth]], axis=-1)
    return jnp.pad(wrapped, ((0, 0), (pad_depth, pad_depth), (0, 0)))


def reference(background, decay_sq, edge_weight, coupling, obs_tiles, obs_values, obs_weights, obs_counts, swath_ids, swath_scale, tile_owner, tile_slot):
    weights_pad = pad_grid(edge_weight, 1)

    def prior_apply(field_in):
        first_pass = stencil(pad_grid(field_in, 1), weights_pad, decay_sq)
        return stencil(pad_grid(mix_fields(coupling, first_pass), 1), weights_pad, decay_sq)

    tile_index = jnp.arange(TILES).astype(jnp.int32)
    block_row = (tile_index // TILE_DEV) % ROW_DEVS
    per_field = CLAT * CLON // PATCH
    per_row = CLON // PATCH
    field_of = tile_slot // per_field
    lat_of = block_row * CLAT + (tile_slot % per_field) // per_row
    lon_of = tile_owner * per_row + tile_slot % per_row

    lookup = jnp.sum(jnp.where(swath_ids[:, None] == jnp.arange(SWATHS)[None, :], swath_scale[None, :], 0.0), axis=1)
    live_rows = jnp.arange(OBS)[None, :] < obs_counts[:, None]
    weight_eff = jnp.where(live_rows, obs_weights * lookup[:, None], 0.0)

    tiles_grouped = obs_tiles.reshape(TILES // TILE_DEV, TILE_DEV, OBS, PATCH)

    def tiles_forward(inputs):
        def one_block(block_pair):
            block_tiles, block_inputs = block_pair
            return jnp.einsum("top,tp->to", block_tiles.astype(jnp.float32), block_inputs.astype(jnp.float32))
        return lax.map(one_block, (tiles_grouped, inputs.reshape(-1, TILE_DEV, PATCH))).reshape(TILES, OBS)

    def tiles_adjoint(weighted):
        def one_block(block_pair):
            block_tiles, block_weighted = block_pair
            return jnp.einsum("top,to->tp", block_tiles.astype(jnp.float32), block_weighted.astype(jnp.float32))
        return lax.map(one_block, (tiles_grouped, weighted.reshape(-1, TILE_DEV, OBS))).reshape(TILES, PATCH)

    def place(contribution):
        grid_view = jnp.zeros((F, NLAT, NLON // PATCH, PATCH), jnp.float32)
        grid_view = grid_view.at[field_of, lat_of, lon_of].add(contribution)
        return grid_view.reshape(F, NLAT, NLON)

    def obs_apply(field_in):
        inputs = field_in.reshape(F, NLAT, NLON // PATCH, PATCH)[field_of, lat_of, lon_of].astype(jnp.bfloat16)
        applied = tiles_forward(inputs)
        weighted = (weight_eff * applied).astype(jnp.bfloat16)
        return place(tiles_adjoint(weighted))

    def operate(field_in):
        return prior_apply(field_in) + obs_apply(field_in)

    scaled_obs = (weight_eff * obs_values).astype(jnp.bfloat16)
    right_side = prior_apply(background) + place(tiles_adjoint(scaled_obs))

    solution = jnp.zeros_like(right_side)
    residual = right_side
    direction = right_side
    norm_now = jnp.sum(residual * residual)
    for iteration in range(ITERS):
        applied = operate(direction)
        step_size = norm_now / jnp.sum(direction * applied)
        solution = solution + step_size * direction
        residual = residual - step_size * applied
        norm_next = jnp.sum(residual * residual)
        direction = residual + (norm_next / norm_now) * direction
        norm_now = norm_next
    return solution, residual
```

```python
import functools

import jax
import jax.numpy as jnp
from jax import lax
from jax.experimental import pallas as pl
from jax.experimental.pallas import tpu as pltpu
from jax.sharding import PartitionSpec as P

CAP = 4
ITERS = 3
SLOT_ROWS = 8
EDGE = 128
MESH = pl.DeviceIdType.MESH


def loop(low, high, body):
    if high - low <= 4:
        for k in range(low, high):
            body(k)
    else:
        lax.fori_loop(low, high, lambda k, c: (body(k), c)[1], 0)


def kernel(
    sizes,
    owner_s,
    slot_s,
    counts_s,
    swath_s,
    scale_s,
    coupling_s,
    bg,
    decay,
    edge,
    tiles_hbm,
    obs_values,
    obs_weights,
    sol_out,
    res_out,
    tiles,
    ve,
    hn,
    hs,
    p0,
    p7,
    coef,
    diag,
    pe,
    pn,
    ps_,
    weight,
    ask,
    req,
    gather_oh,
    scatter_oh,
    xs,
    xr,
    xp,
    zs,
    zr,
    qp,
    part,
    parts,
    halo_send,
    halo_recv,
    ex_send,
    ex_recv,
    red_send,
    red_recv,
    load_sem,
):
    lon_n, lat_n, fld_n = sizes
    row_n = lat_n * fld_n
    dev_n = lon_n * row_n
    fields, rows, cols = bg.shape
    tile_n, obs_len, patch = tiles.shape
    ext = cols + 2 * EDGE
    per_row = cols // patch
    patch_n = fields * rows * per_row
    pos_n = lon_n * SLOT_ROWS
    bf16, f32 = jnp.bfloat16, jnp.float32

    my_lon = lax.axis_index("lon")
    my_row = lax.axis_index("lat") * fld_n + lax.axis_index("fld")
    me = my_lon * row_n + my_row

    def device(lon, row):
        return {"lon": lon, "lat": row // fld_n, "fld": row % fld_n}

    west, east = (my_lon + lon_n - 1) % lon_n, (my_lon + 1) % lon_n
    north, south = (my_row + row_n - 1) % row_n, (my_row + 1) % row_n
    has_north = (my_row > 0).astype(f32)
    has_south = (my_row < row_n - 1).astype(f32)

    load = pltpu.make_async_copy(tiles_hbm, tiles, load_sem)
    load.start()

    barrier = pltpu.get_barrier_semaphore()

    def greet(k):
        other = (me + k) % dev_n
        pl.semaphore_signal(
            barrier, inc=1, device_id=device(other // row_n, other % row_n), device_id_type=MESH
        )

    loop(1, dev_n, greet)

    center = pl.ds(EDGE, cols)
    left, right = pl.ds(0, EDGE), pl.ds(EDGE + cols, EDGE)
    first, final = pl.ds(0, EDGE), pl.ds(cols - EDGE, EDGE)

    def halo_copies(h):
        pairs = (
            (ve.at[h, :, :, pl.ds(EDGE, EDGE)], ve.at[h, :, :, right], west, my_row),
            (ve.at[h, :, :, pl.ds(cols, EDGE)], ve.at[h, :, :, left], east, my_row),
            (p0.at[h], hs.at[h, :, center], my_lon, north),
            (p7.at[h], hn.at[h, :, center], my_lon, south),
            (p0.at[h, :, first], hs.at[h, :, right], west, north),
            (p0.at[h, :, final], hs.at[h, :, left], east, north),
            (p7.at[h, :, first], hn.at[h, :, right], west, south),
            (p7.at[h, :, final], hn.at[h, :, left], east, south),
        )
        return [
            pltpu.make_async_remote_copy(
                src_ref=src,
                dst_ref=dst,
                send_sem=halo_send.at[h, k],
                recv_sem=halo_recv.at[h, k],
                device_id=device(lon, row),
                device_id_type=MESH,
            )
            for k, (src, dst, lon, row) in enumerate(pairs)
        ]

    def put_field(h, f, value):
        ve[h, f, :, EDGE : EDGE + cols] = value
        p0[h, f : f + 1, :] = value[0:1]
        p7[h, f : f + 1, :] = value[rows - 1 : rows]

    def halo_start(h):
        for copy in halo_copies(h):
            copy.start()

    def halo_wait(h):
        for copy in halo_copies(h):
            copy.wait_recv()

    def swap_start(number, out, into):
        def send(k):
            to = (my_lon + k) % lon_n
            pltpu.make_async_remote_copy(
                src_ref=out.at[to],
                dst_ref=into.at[my_lon],
                send_sem=ex_send.at[number],
                recv_sem=ex_recv.at[number],
                device_id=device(to, my_row),
                device_id_type=MESH,
            ).start()

        loop(1, lon_n, send)
        into[my_lon] = out[my_lon]

    def swap_wait(sems, number, buffer):
        some = buffer.at[pl.ds(0, lon_n - 1)]
        pltpu.make_async_copy(some, some, sems.at[number]).wait()

    def total_start(number, value):
        part[number] = value
        parts[number, me] = value

        def send(k):
            other = (me + k) % dev_n
            pltpu.make_async_remote_copy(
                src_ref=part.at[number],
                dst_ref=parts.at[number, me],
                send_sem=red_send.at[number],
                recv_sem=red_recv.at[number],
                device_id=device(other // row_n, other % row_n),
                device_id_type=MESH,
            ).start()

        loop(1, dev_n, send)

    def total_wait(sems, number):
        some = parts.at[number, pl.ds(0, dev_n - 1)]
        pltpu.make_async_copy(some, some, sems.at[number]).wait()

    def total(number):
        total_wait(red_recv, number)
        lanes = jnp.sum(parts[number], axis=0)
        return jnp.sum(lanes, axis=1, keepdims=True)

    def lanes_of(value):
        lane_sum = value[:, 0:128]
        for k in range(1, value.shape[1] // 128):
            lane_sum = lane_sum + value[:, k * 128 : (k + 1) * 128]
        return jnp.sum(lane_sum, axis=0, keepdims=True)

    sub = lax.broadcasted_iota(jnp.int32, (rows, ext), 0)

    def above(value, halo):
        return jnp.where(sub == 0, halo, pltpu.roll(value, 1, 0))

    def below(value, halo):
        return jnp.where(sub == rows - 1, halo, pltpu.roll(value, rows - 1, 0))

    def apply_l(f, value, up_halo, down_halo):
        up, down = above(value, up_halo), below(value, down_halo)
        toward_east = coef[0] * value + coef[1] * up + coef[2] * down
        toward_west = coef[3] * value + coef[4] * up + coef[5] * down
        result = diag[f] * value - coef[6] * up - coef[7] * down
        result = result - pltpu.roll(toward_east, ext - 1, 1) - pltpu.roll(toward_west, 1, 1)
        return result[:, EDGE : EDGE + cols]

    def mixed(first_pass, f):
        acc = coupling_s[f, 0] * first_pass[0]
        for g in range(1, fields):
            acc = acc + coupling_s[f, g] * first_pass[g]
        return acc

    def split3(value):
        high = value.astype(bf16)
        rest = value - high.astype(f32)
        middle = rest.astype(bf16)
        return high, middle, (rest - middle.astype(f32)).astype(bf16)

    row_iota = lax.broadcasted_iota(jnp.int32, (pos_n, 128), 0)
    wide_iota = lax.broadcasted_iota(jnp.int32, (pos_n, patch), 0)
    obs_iota = lax.broadcasted_iota(jnp.int32, (pos_n, obs_len), 1)

    for f in range(fields):
        put_field(0, f, bg[f])
    for e in range(4):
        put_field(1, e, edge[e])

    positions = []
    for t in range(tile_n):
        rank = jnp.int32(0)
        for other in range(t):
            rank = rank + (owner_s[other] == owner_s[t]).astype(jnp.int32)
        positions.append(owner_s[t] * SLOT_ROWS + rank)

    asked = jnp.full((pos_n, 128), -1, jnp.int32)
    weight_all = jnp.zeros((pos_n, obs_len), f32)
    values_all = jnp.zeros((pos_n, obs_len), f32)
    for t in range(tile_n):
        number = slot_s[t]
        column, rest = number % per_row, number // per_row
        moved = (column * fields + rest // rows) * rows + rest % rows
        asked = jnp.where(row_iota == positions[t], moved, asked)
        here = wide_iota == positions[t]
        live = here & (obs_iota < counts_s[t])
        weight_all = jnp.where(
            live, obs_weights[t : t + 1, :] * scale_s[swath_s[t]], weight_all
        )
        values_all = jnp.where(here, obs_values[t : t + 1, :], values_all)
    ask[...] = asked.reshape(lon_n, SLOT_ROWS, 128)
    weight[...] = weight_all

    def spread(value, t):
        return jnp.where(wide_iota == positions[t], value, 0.0).astype(bf16)

    def forward(value):
        acc = None
        for t in range(tile_n):
            term = lax.dot_general(
                spread(value, t), tiles[t], (((1,), (1,)), ((), ())), preferred_element_type=f32
            )
            acc = term if acc is None else acc + term
        return acc

    def adjoint(value):
        acc = None
        for t in range(tile_n):
            term = lax.dot_general(
                spread(value, t), tiles[t], (((1,), (0,)), ((), ())), preferred_element_type=f32
            )
            acc = term if acc is None else acc + term
        return acc

    pl.semaphore_wait(barrier, dev_n - 1)
    halo_start(1)
    halo_start(0)
    swap_start(0, ask, req)

    load.wait()
    scaled = (weight_all * values_all).astype(bf16).astype(f32)
    zs[0] = adjoint(scaled).reshape(lon_n, SLOT_ROWS, patch)
    swap_start(1, zs.at[0], zr.at[0])

    halo_wait(1)
    w = [ve[1, e] for e in range(4)]
    w_up = [above(w[e], hn[1, e : e + 1, :] * has_north) for e in range(4)]
    w_down = [below(w[e], hs[1, e : e + 1, :] * has_south) for e in range(4)]
    w_west = {e: pltpu.roll(w[e], 1, 1) for e in (0, 2, 3)}
    w_east = {e: pltpu.roll(w[e], ext - 1, 1) for e in (0, 2, 3)}
    e0, e1, e2 = (
        0.5 * (w_west[0] + w[0]),
        0.5 * (w_west[3] + w_up[3]),
        0.5 * (w_west[2] + w_down[2]),
    )
    v0, v1, v2 = (
        0.5 * (w_east[0] + w[0]),
        0.5 * (w_east[2] + w_up[2]),
        0.5 * (w_east[3] + w_down[3]),
    )
    n0, n1 = 0.5 * (w[1] + w_up[1]), 0.5 * (w[1] + w_down[1])
    for k, value in enumerate((e0, e1, e2, v0, v1, v2, n0, n1)):
        coef[k] = value
    degree = n0 + n1 + pltpu.roll(e0 + e1 + e2, ext - 1, 1) + pltpu.roll(v0 + v1 + v2, 1, 1)
    for f in range(fields):
        diag[f] = degree
        diag[f, :, EDGE : EDGE + cols] = decay[f] + degree[:, EDGE : EDGE + cols]

    def up_of(h, f):
        return hn[h, f : f + 1, :] * has_north

    def down_of(h, f):
        return hs[h, f : f + 1, :] * has_south

    halo_wait(0)
    first_pass = [apply_l(f, ve[0, f], up_of(0, f), down_of(0, f)) for f in range(fields)]
    for f in range(fields):
        put_field(2, f, mixed(first_pass, f))
    halo_start(2)

    swap_wait(ex_recv, 0, req)
    wanted = req[...].reshape(pos_n, 128)
    wanted = jnp.concatenate([wanted] * (patch_n // 128), axis=1)
    picked = wanted == lax.broadcasted_iota(jnp.int32, (pos_n, patch_n), 1)
    chosen = jnp.where(picked, 1.0, 0.0)
    gather_oh[...] = chosen.astype(bf16)
    if pos_n < 128:
        chosen = jnp.concatenate([chosen, jnp.zeros((128 - pos_n, patch_n), f32)], axis=0)
    scatter_oh[...] = chosen.T.astype(bf16)

    def placed(number):
        arrived = zr[number].reshape(pos_n, patch)
        if pos_n < 128:
            arrived = jnp.concatenate([arrived, jnp.zeros((128 - pos_n, patch), f32)], axis=0)
        high, middle, low = split3(arrived)
        return (
            jnp.dot(scatter_oh[...], low, preferred_element_type=f32)
            + jnp.dot(scatter_oh[...], middle, preferred_element_type=f32)
        ) + jnp.dot(scatter_oh[...], high, preferred_element_type=f32)

    def placed_field(blocks, f):
        return jnp.concatenate(
            [
                blocks[(c * fields + f) * rows : (c * fields + f + 1) * rows]
                for c in range(per_row)
            ],
            axis=1,
        )

    halo_wait(2)
    second = [apply_l(f, ve[2, f], up_of(2, f), down_of(2, f)) for f in range(fields)]
    for f in range(fields):
        qp[f] = second[f]
    swap_wait(ex_recv, 1, zr.at[0])
    blocks = placed(0)
    for f in range(fields):
        put_field(3, f, qp[f] + placed_field(blocks, f))
        sol_out[f] = jnp.zeros((rows, cols), f32)
    pe[...] = jnp.zeros_like(pe)
    pn[...] = jnp.zeros_like(pn)
    ps_[...] = jnp.zeros_like(ps_)
    xp[...] = jnp.zeros_like(xp)

    def iterate(it, norm_before):
        h_r, h_u = 3 + 2 * it, 4 + 2 * it
        halo_start(h_r)
        squares = jnp.zeros((1, 128), f32)
        for f in range(fields):
            value = ve[h_r, f, :, EDGE : EDGE + cols]
            squares = squares + lanes_of(value * value)
        total_start(2 * it, squares)
        stacked = jnp.concatenate(
            [
                ve[h_r, f, :, EDGE + c * patch : EDGE + (c + 1) * patch]
                for c in range(per_row)
                for f in range(fields)
            ],
            axis=0,
        )
        high, middle, low = split3(stacked)
        patches = (
            jnp.dot(gather_oh[...], low, preferred_element_type=f32)
            + jnp.dot(gather_oh[...], middle, preferred_element_type=f32)
        ) + jnp.dot(gather_oh[...], high, preferred_element_type=f32)
        xs[it] = patches.reshape(lon_n, SLOT_ROWS, patch)
        swap_start(2 + 2 * it, xs.at[it], xr.at[it])

        halo_wait(h_r)
        swap_wait(ex_recv, 2 + 2 * it, xr.at[it])
        norm = total(2 * it)
        ratio = norm / norm_before
        for f in range(fields):
            pe[f] = ve[h_r, f] + ratio * pe[f]
        pn[...] = hn[h_r] * has_north + ratio * pn[...]
        ps_[...] = hs[h_r] * has_south + ratio * ps_[...]
        seen = xr[it].reshape(pos_n, patch) + ratio * xp[...]
        xp[...] = seen

        first_pass = [
            apply_l(f, pe[f], pn[f : f + 1, :], ps_[f : f + 1, :]) for f in range(fields)
        ]
        curve = jnp.zeros((1, 128), f32)
        for f in range(fields):
            value = mixed(first_pass, f)
            put_field(h_u, f, value)
            curve = curve + lanes_of(value * first_pass[f])
        halo_start(h_u)

        applied = forward(seen)
        weighted = (weight[...] * applied).astype(bf16).astype(f32)
        curve = curve + lanes_of(applied * weighted)
        total_start(2 * it + 1, curve)
        zs[it + 1] = adjoint(weighted).reshape(lon_n, SLOT_ROWS, patch)
        swap_start(3 + 2 * it, zs.at[it + 1], zr.at[it + 1])

        halo_wait(h_u)
        for f in range(fields):
            qp[f] = apply_l(f, ve[h_u, f], up_of(h_u, f), down_of(h_u, f))
        swap_wait(ex_recv, 3 + 2 * it, zr.at[it + 1])
        blocks = placed(it + 1)
        step = norm / total(2 * it + 1)
        for f in range(fields):
            sol_out[f] = sol_out[f] + step * pe[f, :, EDGE : EDGE + cols]
            image = qp[f] + placed_field(blocks, f)
            put_field(h_r + 2, f, ve[h_r, f, :, EDGE : EDGE + cols] - step * image)
        return norm

    lax.fori_loop(0, ITERS, iterate, jnp.full((1, 1), 1.0, f32))
    for f in range(fields):
        res_out[f] = ve[3 + 2 * ITERS, f, :, EDGE : EDGE + cols]

    def sent_halo(h, carry):
        for copy in halo_copies(h):
            copy.wait_send()
        return carry

    lax.fori_loop(0, 3 + 2 * ITERS, sent_halo, 0)
    swap_wait(ex_send, 0, req)
    swap_wait(ex_send, 1, zr.at[0])

    def sent_rest(it, carry):
        swap_wait(ex_send, 2 + 2 * it, xr.at[it])
        swap_wait(ex_send, 3 + 2 * it, zr.at[it + 1])
        total_wait(red_send, 2 * it)
        total_wait(red_send, 2 * it + 1)
        return carry

    lax.fori_loop(0, ITERS, sent_rest, 0)


def on_device(
    sizes,
    background,
    decay_sq,
    edge_weight,
    coupling,
    obs_tiles,
    obs_values,
    obs_weights,
    obs_counts,
    swath_ids,
    swath_scale,
    tile_owner,
    tile_slot,
):
    fields, rows, cols = background.shape
    tile_n, obs_len, patch = obs_tiles.shape
    lon_n, lat_n, fld_n = sizes
    dev_n = lon_n * lat_n * fld_n
    ext = cols + 2 * EDGE
    pos_n = lon_n * SLOT_ROWS
    patch_n = fields * rows * cols // patch
    halos = 4 + 2 * ITERS
    f32, bf16 = jnp.float32, jnp.bfloat16
    smem = pl.BlockSpec(memory_space=pltpu.SMEM)
    vmem = pl.BlockSpec(memory_space=pltpu.VMEM)
    dma = pltpu.SemaphoreType.DMA
    shape = jax.ShapeDtypeStruct((fields, rows, cols), f32)
    return pl.pallas_call(
        functools.partial(kernel, sizes),
        out_shape=(shape, shape),
        in_specs=[smem] * 6 + [vmem] * 3 + [pl.BlockSpec(memory_space=pl.ANY)] + [vmem] * 2,
        out_specs=(vmem, vmem),
        scratch_shapes=[
            pltpu.VMEM((tile_n, obs_len, patch), bf16),
            pltpu.VMEM((halos, fields, rows, ext), f32),
            pltpu.VMEM((halos, fields, ext), f32),
            pltpu.VMEM((halos, fields, ext), f32),
            pltpu.VMEM((halos, fields, cols), f32),
            pltpu.VMEM((halos, fields, cols), f32),
            pltpu.VMEM((8, rows, ext), f32),
            pltpu.VMEM((fields, rows, ext), f32),
            pltpu.VMEM((fields, rows, ext), f32),
            pltpu.VMEM((fields, ext), f32),
            pltpu.VMEM((fields, ext), f32),
            pltpu.VMEM((pos_n, obs_len), f32),
            pltpu.VMEM((lon_n, SLOT_ROWS, 128), jnp.int32),
            pltpu.VMEM((lon_n, SLOT_ROWS, 128), jnp.int32),
            pltpu.VMEM((pos_n, patch_n), bf16),
            pltpu.VMEM((patch_n, 128), bf16),
            pltpu.VMEM((ITERS, lon_n, SLOT_ROWS, patch), f32),
            pltpu.VMEM((ITERS, lon_n, SLOT_ROWS, patch), f32),
            pltpu.VMEM((pos_n, patch), f32),
            pltpu.VMEM((ITERS + 1, lon_n, SLOT_ROWS, patch), f32),
            pltpu.VMEM((ITERS + 1, lon_n, SLOT_ROWS, patch), f32),
            pltpu.VMEM((fields, rows, cols), f32),
            pltpu.VMEM((2 * ITERS, 1, 128), f32),
            pltpu.VMEM((2 * ITERS, dev_n, 1, 128), f32),
            dma((halos, 8)),
            dma((halos, 8)),
            dma((2 + 2 * ITERS,)),
            dma((2 + 2 * ITERS,)),
            dma((2 * ITERS,)),
            dma((2 * ITERS,)),
            dma(()),
        ],
        compiler_params=pltpu.CompilerParams(
            collective_id=0, has_side_effects=True, vmem_limit_bytes=40 * 1024 * 1024
        ),
    )(
        tile_owner,
        tile_slot,
        obs_counts,
        swath_ids,
        swath_scale,
        coupling,
        background,
        decay_sq,
        edge_weight,
        obs_tiles,
        obs_values,
        obs_weights,
    )


def solution(mesh):
    sizes = (mesh.shape["lon"], mesh.shape["lat"], mesh.shape["fld"])
    return jax.shard_map(
        functools.partial(on_device, sizes),
        mesh=mesh,
        in_specs=(
            P("group", ("lat", "fld"), "lon"),
            P(None, ("lat", "fld"), "lon"),
            P(None, ("lat", "fld"), "lon"),
            P(),
            P(("lon", "lat", "fld"), None, None),
            P(("group", "lon", "lat", "fld"), None),
            P(("lon", "lat", "fld"), None),
            P(("lon", "lat", "fld")),
            P(("lon", "lat", "fld")),
            P(),
            P(("lon", "lat", "fld")),
            P(("lon", "lat", "fld")),
        ),
        out_specs=(P("group", ("lat", "fld"), "lon"), P("group", ("lat", "fld"), "lon")),
        check_vma=False,
    )
```

```python
import functools

import jax
import jax.numpy as jnp
from jax import lax
from jax.experimental import pallas as pl
from jax.experimental.pallas import tpu as pltpu
from jax.sharding import PartitionSpec as P

CAP = 4
ITERS = 3
SLOT_ROWS = 8
EDGE = 128
MESH = pl.DeviceIdType.MESH


def loop(low, high, body):
    if high - low <= 4:
        for k in range(low, high):
            body(k)
    else:
        lax.fori_loop(low, high, lambda k, c: (body(k), c)[1], 0)


def kernel(
    sizes,
    owner_hbm,
    slot_hbm,
    counts_hbm,
    swath_hbm,
    scale_hbm,
    coupling_hbm,
    bg_hbm,
    decay_hbm,
    edge_hbm,
    tiles_hbm,
    values_hbm,
    weights_hbm,
    sol_out,
    res_out,
    owner_s,
    slot_s,
    counts_s,
    swath_s,
    scale_s,
    coupling_s,
    bg,
    decay,
    edge,
    obs_values,
    obs_weights,
    tiles,
    ve,
    hn,
    hs,
    p0,
    p7,
    coef,
    diag,
    pe,
    pn,
    ps_,
    weight,
    ask,
    req,
    gather_oh,
    scatter_oh,
    xs,
    xr,
    xp,
    zs,
    zr,
    qp,
    part,
    parts,
    halo_send,
    halo_recv,
    ex_send,
    ex_recv,
    red_send,
    red_recv,
    load_sem,
):
    lon_n, lat_n, fld_n = sizes
    row_n = lat_n * fld_n
    dev_n = lon_n * row_n
    fields, rows, cols = bg.shape
    tile_n, obs_len, patch = tiles.shape
    ext = cols + 2 * EDGE
    per_row = cols // patch
    patch_n = fields * rows * per_row
    pos_n = lon_n * SLOT_ROWS
    bf16, f32 = jnp.bfloat16, jnp.float32

    my_lon = lax.axis_index("lon")
    my_row = lax.axis_index("lat") * fld_n + lax.axis_index("fld")
    me = my_lon * row_n + my_row

    def device(lon, row):
        return {"lon": lon, "lat": row // fld_n, "fld": row % fld_n}

    west, east = (my_lon + lon_n - 1) % lon_n, (my_lon + 1) % lon_n
    north, south = (my_row + row_n - 1) % row_n, (my_row + 1) % row_n
    has_north = (my_row > 0).astype(f32)
    has_south = (my_row < row_n - 1).astype(f32)

    loads = [
        pltpu.make_async_copy(src, dst, load_sem.at[k])
        for k, (src, dst) in enumerate(
            (
                (edge_hbm, edge),
                (bg_hbm, bg),
                (owner_hbm, owner_s),
                (slot_hbm, slot_s),
                (counts_hbm, counts_s),
                (swath_hbm, swath_s),
                (scale_hbm, scale_s),
                (coupling_hbm, coupling_s),
                (values_hbm, obs_values),
                (weights_hbm, obs_weights),
                (decay_hbm, decay),
                (tiles_hbm, tiles),
            )
        )
    ]
    for load in loads:
        load.start()

    barrier = pltpu.get_barrier_semaphore()

    def greet(k):
        other = (me + k) % dev_n
        pl.semaphore_signal(
            barrier, inc=1, device_id=device(other // row_n, other % row_n), device_id_type=MESH
        )

    loop(1, dev_n, greet)

    center = pl.ds(EDGE, cols)
    left, right = pl.ds(0, EDGE), pl.ds(EDGE + cols, EDGE)
    first, final = pl.ds(0, EDGE), pl.ds(cols - EDGE, EDGE)

    def halo_copies(h):
        pairs = (
            (ve.at[h, :, :, pl.ds(EDGE, EDGE)], ve.at[h, :, :, right], west, my_row),
            (ve.at[h, :, :, pl.ds(cols, EDGE)], ve.at[h, :, :, left], east, my_row),
            (p0.at[h], hs.at[h, :, center], my_lon, north),
            (p7.at[h], hn.at[h, :, center], my_lon, south),
            (p0.at[h, :, first], hs.at[h, :, right], west, north),
            (p0.at[h, :, final], hs.at[h, :, left], east, north),
            (p7.at[h, :, first], hn.at[h, :, right], west, south),
            (p7.at[h, :, final], hn.at[h, :, left], east, south),
        )
        return [
            pltpu.make_async_remote_copy(
                src_ref=src,
                dst_ref=dst,
                send_sem=halo_send.at[h, k],
                recv_sem=halo_recv.at[h, k],
                device_id=device(lon, row),
                device_id_type=MESH,
            )
            for k, (src, dst, lon, row) in enumerate(pairs)
        ]

    def put_field(h, f, value):
        ve[h, f, :, EDGE : EDGE + cols] = value
        p0[h, f : f + 1, :] = value[0:1]
        p7[h, f : f + 1, :] = value[rows - 1 : rows]

    def halo_start(h):
        for copy in halo_copies(h):
            copy.start()

    def halo_wait(h):
        for copy in halo_copies(h):
            copy.wait_recv()

    def swap_start(number, out, into):
        def send(k):
            to = (my_lon + k) % lon_n
            pltpu.make_async_remote_copy(
                src_ref=out.at[to],
                dst_ref=into.at[my_lon],
                send_sem=ex_send.at[number],
                recv_sem=ex_recv.at[number],
                device_id=device(to, my_row),
                device_id_type=MESH,
            ).start()

        loop(1, lon_n, send)
        into[my_lon] = out[my_lon]

    def swap_wait(sems, number, buffer):
        some = buffer.at[pl.ds(0, lon_n - 1)]
        pltpu.make_async_copy(some, some, sems.at[number]).wait()

    def total_start(number, value):
        part[number] = value
        parts[number, me] = value

        def send(k):
            other = (me + k) % dev_n
            pltpu.make_async_remote_copy(
                src_ref=part.at[number],
                dst_ref=parts.at[number, me],
                send_sem=red_send.at[number],
                recv_sem=red_recv.at[number],
                device_id=device(other // row_n, other % row_n),
                device_id_type=MESH,
            ).start()

        loop(1, dev_n, send)

    def total_wait(sems, number):
        some = parts.at[number, pl.ds(0, dev_n - 1)]
        pltpu.make_async_copy(some, some, sems.at[number]).wait()

    def total(number):
        total_wait(red_recv, number)
        lanes = jnp.sum(parts[number], axis=0)
        return jnp.sum(lanes, axis=1, keepdims=True)

    def lanes_of(value):
        lane_sum = value[:, 0:128]
        for k in range(1, value.shape[1] // 128):
            lane_sum = lane_sum + value[:, k * 128 : (k + 1) * 128]
        return jnp.sum(lane_sum, axis=0, keepdims=True)

    sub = lax.broadcasted_iota(jnp.int32, (rows, ext), 0)

    def above(value, halo):
        return jnp.where(sub == 0, halo, pltpu.roll(value, 1, 0))

    def below(value, halo):
        return jnp.where(sub == rows - 1, halo, pltpu.roll(value, rows - 1, 0))

    def apply_l(f, value, up_halo, down_halo):
        up, down = above(value, up_halo), below(value, down_halo)
        toward_east = coef[0] * value + coef[1] * up + coef[2] * down
        toward_west = coef[3] * value + coef[4] * up + coef[5] * down
        result = diag[f] * value - coef[6] * up - coef[7] * down
        result = result - pltpu.roll(toward_east, ext - 1, 1) - pltpu.roll(toward_west, 1, 1)
        return result[:, EDGE : EDGE + cols]

    def mixed(first_pass, f):
        acc = coupling_s[f, 0] * first_pass[0]
        for g in range(1, fields):
            acc = acc + coupling_s[f, g] * first_pass[g]
        return acc

    def split3(value):
        high = value.astype(bf16)
        rest = value - high.astype(f32)
        middle = rest.astype(bf16)
        return high, middle, (rest - middle.astype(f32)).astype(bf16)

    row_iota = lax.broadcasted_iota(jnp.int32, (pos_n, 128), 0)
    wide_iota = lax.broadcasted_iota(jnp.int32, (pos_n, patch), 0)
    obs_iota = lax.broadcasted_iota(jnp.int32, (pos_n, obs_len), 1)

    loads[0].wait()
    for e in range(4):
        put_field(1, e, edge[e])
    loads[1].wait()
    for f in range(fields):
        put_field(0, f, bg[f])

    def spread(value, t):
        return jnp.where(wide_iota == positions[t], value, 0.0).astype(bf16)

    def forward(value):
        acc = None
        for t in range(tile_n):
            term = lax.dot_general(
                spread(value, t), tiles[t], (((1,), (1,)), ((), ())), preferred_element_type=f32
            )
            acc = term if acc is None else acc + term
        return acc

    def adjoint(value):
        acc = None
        for t in range(tile_n):
            term = lax.dot_general(
                spread(value, t), tiles[t], (((1,), (0,)), ((), ())), preferred_element_type=f32
            )
            acc = term if acc is None else acc + term
        return acc

    pl.semaphore_wait(barrier, dev_n - 1)
    halo_start(1)
    halo_start(0)

    for load in loads[2:11]:
        load.wait()
    positions = []
    for t in range(tile_n):
        rank = jnp.int32(0)
        for other in range(t):
            rank = rank + (owner_s[other] == owner_s[t]).astype(jnp.int32)
        positions.append(owner_s[t] * SLOT_ROWS + rank)

    asked = jnp.full((pos_n, 128), -1, jnp.int32)
    weight_all = jnp.zeros((pos_n, obs_len), f32)
    values_all = jnp.zeros((pos_n, obs_len), f32)
    for t in range(tile_n):
        number = slot_s[t]
        column, rest = number % per_row, number // per_row
        moved = (column * fields + rest // rows) * rows + rest % rows
        asked = jnp.where(row_iota == positions[t], moved, asked)
        here = wide_iota == positions[t]
        live = here & (obs_iota < counts_s[t])
        weight_all = jnp.where(
            live, obs_weights[t : t + 1, :] * scale_s[swath_s[t]], weight_all
        )
        values_all = jnp.where(here, obs_values[t : t + 1, :], values_all)
    ask[...] = asked.reshape(lon_n, SLOT_ROWS, 128)
    weight[...] = weight_all

    swap_start(0, ask, req)

    loads[11].wait()
    scaled = (weight_all * values_all).astype(bf16).astype(f32)
    zs[0] = adjoint(scaled).reshape(lon_n, SLOT_ROWS, patch)
    swap_start(1, zs.at[0], zr.at[0])

    halo_wait(1)
    w = [ve[1, e] for e in range(4)]
    w_up = [above(w[e], hn[1, e : e + 1, :] * has_north) for e in range(4)]
    w_down = [below(w[e], hs[1, e : e + 1, :] * has_south) for e in range(4)]
    w_west = {e: pltpu.roll(w[e], 1, 1) for e in (0, 2, 3)}
    w_east = {e: pltpu.roll(w[e], ext - 1, 1) for e in (0, 2, 3)}
    e0, e1, e2 = (
        0.5 * (w_west[0] + w[0]),
        0.5 * (w_west[3] + w_up[3]),
        0.5 * (w_west[2] + w_down[2]),
    )
    v0, v1, v2 = (
        0.5 * (w_east[0] + w[0]),
        0.5 * (w_east[2] + w_up[2]),
        0.5 * (w_east[3] + w_down[3]),
    )
    n0, n1 = 0.5 * (w[1] + w_up[1]), 0.5 * (w[1] + w_down[1])
    for k, value in enumerate((e0, e1, e2, v0, v1, v2, n0, n1)):
        coef[k] = value
    degree = n0 + n1 + pltpu.roll(e0 + e1 + e2, ext - 1, 1) + pltpu.roll(v0 + v1 + v2, 1, 1)
    for f in range(fields):
        diag[f] = degree
        diag[f, :, EDGE : EDGE + cols] = decay[f] + degree[:, EDGE : EDGE + cols]

    def up_of(h, f):
        return hn[h, f : f + 1, :] * has_north

    def down_of(h, f):
        return hs[h, f : f + 1, :] * has_south

    halo_wait(0)
    first_pass = [apply_l(f, ve[0, f], up_of(0, f), down_of(0, f)) for f in range(fields)]
    for f in range(fields):
        put_field(2, f, mixed(first_pass, f))
    halo_start(2)

    swap_wait(ex_recv, 0, req)
    wanted = req[...].reshape(pos_n, 128)
    wanted = jnp.concatenate([wanted] * (patch_n // 128), axis=1)
    picked = wanted == lax.broadcasted_iota(jnp.int32, (pos_n, patch_n), 1)
    chosen = jnp.where(picked, 1.0, 0.0)
    gather_oh[...] = chosen.astype(bf16)
    if pos_n < 128:
        chosen = jnp.concatenate([chosen, jnp.zeros((128 - pos_n, patch_n), f32)], axis=0)
    scatter_oh[...] = chosen.T.astype(bf16)

    def placed(number):
        arrived = zr[number].reshape(pos_n, patch)
        if pos_n < 128:
            arrived = jnp.concatenate([arrived, jnp.zeros((128 - pos_n, patch), f32)], axis=0)
        high, middle, low = split3(arrived)
        return (
            jnp.dot(scatter_oh[...], low, preferred_element_type=f32)
            + jnp.dot(scatter_oh[...], middle, preferred_element_type=f32)
        ) + jnp.dot(scatter_oh[...], high, preferred_element_type=f32)

    def placed_field(blocks, f):
        return jnp.concatenate(
            [
                blocks[(c * fields + f) * rows : (c * fields + f + 1) * rows]
                for c in range(per_row)
            ],
            axis=1,
        )

    halo_wait(2)
    second = [apply_l(f, ve[2, f], up_of(2, f), down_of(2, f)) for f in range(fields)]
    for f in range(fields):
        qp[f] = second[f]
    swap_wait(ex_recv, 1, zr.at[0])
    blocks = placed(0)
    for f in range(fields):
        put_field(3, f, qp[f] + placed_field(blocks, f))
        sol_out[f] = jnp.zeros((rows, cols), f32)
    pe[...] = jnp.zeros_like(pe)
    pn[...] = jnp.zeros_like(pn)
    ps_[...] = jnp.zeros_like(ps_)
    xp[...] = jnp.zeros_like(xp)

    def iterate(it, norm_before):
        h_r, h_u = 3 + 2 * it, 4 + 2 * it
        halo_start(h_r)
        squares = jnp.zeros((1, 128), f32)
        for f in range(fields):
            value = ve[h_r, f, :, EDGE : EDGE + cols]
            squares = squares + lanes_of(value * value)
        total_start(2 * it, squares)
        stacked = jnp.concatenate(
            [
                ve[h_r, f, :, EDGE + c * patch : EDGE + (c + 1) * patch]
                for c in range(per_row)
                for f in range(fields)
            ],
            axis=0,
        )
        high, middle, low = split3(stacked)
        patches = (
            jnp.dot(gather_oh[...], low, preferred_element_type=f32)
            + jnp.dot(gather_oh[...], middle, preferred_element_type=f32)
        ) + jnp.dot(gather_oh[...], high, preferred_element_type=f32)
        xs[it] = patches.reshape(lon_n, SLOT_ROWS, patch)
        swap_start(2 + 2 * it, xs.at[it], xr.at[it])

        halo_wait(h_r)
        swap_wait(ex_recv, 2 + 2 * it, xr.at[it])
        norm = total(2 * it)
        ratio = norm / norm_before
        for f in range(fields):
            pe[f] = ve[h_r, f] + ratio * pe[f]
        pn[...] = hn[h_r] * has_north + ratio * pn[...]
        ps_[...] = hs[h_r] * has_south + ratio * ps_[...]
        seen = xr[it].reshape(pos_n, patch) + ratio * xp[...]
        xp[...] = seen

        first_pass = [
            apply_l(f, pe[f], pn[f : f + 1, :], ps_[f : f + 1, :]) for f in range(fields)
        ]
        curve = jnp.zeros((1, 128), f32)
        for f in range(fields):
            value = mixed(first_pass, f)
            put_field(h_u, f, value)
            curve = curve + lanes_of(value * first_pass[f])
        halo_start(h_u)

        applied = forward(seen)
        weighted = (weight[...] * applied).astype(bf16).astype(f32)
        curve = curve + lanes_of(applied * weighted)
        total_start(2 * it + 1, curve)
        zs[it + 1] = adjoint(weighted).reshape(lon_n, SLOT_ROWS, patch)
        swap_start(3 + 2 * it, zs.at[it + 1], zr.at[it + 1])

        halo_wait(h_u)
        for f in range(fields):
            qp[f] = apply_l(f, ve[h_u, f], up_of(h_u, f), down_of(h_u, f))
        swap_wait(ex_recv, 3 + 2 * it, zr.at[it + 1])
        blocks = placed(it + 1)
        step = norm / total(2 * it + 1)
        for f in range(fields):
            sol_out[f] = sol_out[f] + step * pe[f, :, EDGE : EDGE + cols]
            image = qp[f] + placed_field(blocks, f)
            put_field(h_r + 2, f, ve[h_r, f, :, EDGE : EDGE + cols] - step * image)
        return norm

    lax.fori_loop(0, ITERS, iterate, jnp.full((1, 1), 1.0, f32))
    for f in range(fields):
        res_out[f] = ve[3 + 2 * ITERS, f, :, EDGE : EDGE + cols]

    def sent_halo(h, carry):
        for copy in halo_copies(h):
            copy.wait_send()
        return carry

    lax.fori_loop(0, 3 + 2 * ITERS, sent_halo, 0)
    swap_wait(ex_send, 0, req)
    swap_wait(ex_send, 1, zr.at[0])

    def sent_rest(it, carry):
        swap_wait(ex_send, 2 + 2 * it, xr.at[it])
        swap_wait(ex_send, 3 + 2 * it, zr.at[it + 1])
        total_wait(red_send, 2 * it)
        total_wait(red_send, 2 * it + 1)
        return carry

    lax.fori_loop(0, ITERS, sent_rest, 0)


def on_device(
    sizes,
    background,
    decay_sq,
    edge_weight,
    coupling,
    obs_tiles,
    obs_values,
    obs_weights,
    obs_counts,
    swath_ids,
    swath_scale,
    tile_owner,
    tile_slot,
):
    fields, rows, cols = background.shape
    tile_n, obs_len, patch = obs_tiles.shape
    lon_n, lat_n, fld_n = sizes
    dev_n = lon_n * lat_n * fld_n
    ext = cols + 2 * EDGE
    pos_n = lon_n * SLOT_ROWS
    patch_n = fields * rows * cols // patch
    halos = 4 + 2 * ITERS
    f32, bf16 = jnp.float32, jnp.bfloat16
    vmem = pl.BlockSpec(memory_space=pltpu.VMEM)
    dma = pltpu.SemaphoreType.DMA
    shape = jax.ShapeDtypeStruct((fields, rows, cols), f32)
    return pl.pallas_call(
        functools.partial(kernel, sizes),
        out_shape=(shape, shape),
        in_specs=[pl.BlockSpec(memory_space=pltpu.HBM)] * 12,
        out_specs=(vmem, vmem),
        scratch_shapes=[
            pltpu.SMEM(tile_owner.shape, jnp.int32),
            pltpu.SMEM(tile_slot.shape, jnp.int32),
            pltpu.SMEM(obs_counts.shape, jnp.int32),
            pltpu.SMEM(swath_ids.shape, jnp.int32),
            pltpu.SMEM(swath_scale.shape, f32),
            pltpu.SMEM(coupling.shape, f32),
            pltpu.VMEM(background.shape, f32),
            pltpu.VMEM(decay_sq.shape, f32),
            pltpu.VMEM(edge_weight.shape, f32),
            pltpu.VMEM(obs_values.shape, f32),
            pltpu.VMEM(obs_weights.shape, f32),
            pltpu.VMEM((tile_n, obs_len, patch), bf16),
            pltpu.VMEM((halos, fields, rows, ext), f32),
            pltpu.VMEM((halos, fields, ext), f32),
            pltpu.VMEM((halos, fields, ext), f32),
            pltpu.VMEM((halos, fields, cols), f32),
            pltpu.VMEM((halos, fields, cols), f32),
            pltpu.VMEM((8, rows, ext), f32),
            pltpu.VMEM((fields, rows, ext), f32),
            pltpu.VMEM((fields, rows, ext), f32),
            pltpu.VMEM((fields, ext), f32),
            pltpu.VMEM((fields, ext), f32),
            pltpu.VMEM((pos_n, obs_len), f32),
            pltpu.VMEM((lon_n, SLOT_ROWS, 128), jnp.int32),
            pltpu.VMEM((lon_n, SLOT_ROWS, 128), jnp.int32),
            pltpu.VMEM((pos_n, patch_n), bf16),
            pltpu.VMEM((patch_n, 128), bf16),
            pltpu.VMEM((ITERS, lon_n, SLOT_ROWS, patch), f32),
            pltpu.VMEM((ITERS, lon_n, SLOT_ROWS, patch), f32),
            pltpu.VMEM((pos_n, patch), f32),
            pltpu.VMEM((ITERS + 1, lon_n, SLOT_ROWS, patch), f32),
            pltpu.VMEM((ITERS + 1, lon_n, SLOT_ROWS, patch), f32),
            pltpu.VMEM((fields, rows, cols), f32),
            pltpu.VMEM((2 * ITERS, 1, 128), f32),
            pltpu.VMEM((2 * ITERS, dev_n, 1, 128), f32),
            dma((halos, 8)),
            dma((halos, 8)),
            dma((2 + 2 * ITERS,)),
            dma((2 + 2 * ITERS,)),
            dma((2 * ITERS,)),
            dma((2 * ITERS,)),
            dma((12,)),
        ],
        compiler_params=pltpu.CompilerParams(
            collective_id=0, has_side_effects=True, vmem_limit_bytes=67043328
        ),
    )(
        tile_owner,
        tile_slot,
        obs_counts,
        swath_ids,
        swath_scale,
        coupling,
        background,
        decay_sq,
        edge_weight,
        obs_tiles,
        obs_values,
        obs_weights,
    )


def solution(mesh):
    sizes = (mesh.shape["lon"], mesh.shape["lat"], mesh.shape["fld"])
    return jax.shard_map(
        functools.partial(on_device, sizes),
        mesh=mesh,
        in_specs=(
            P("group", ("lat", "fld"), "lon"),
            P(None, ("lat", "fld"), "lon"),
            P(None, ("lat", "fld"), "lon"),
            P(),
            P(("lon", "lat", "fld"), None, None),
            P(("group", "lon", "lat", "fld"), None),
            P(("lon", "lat", "fld"), None),
            P(("lon", "lat", "fld")),
            P(("lon", "lat", "fld")),
            P(),
            P(("lon", "lat", "fld")),
            P(("lon", "lat", "fld")),
        ),
        out_specs=(P("group", ("lat", "fld"), "lon"), P("group", ("lat", "fld"), "lon")),
        check_vma=False,
    )
```

```python
import functools

import jax
import jax.numpy as jnp
from jax import lax
from jax.experimental import pallas as pl
from jax.experimental.pallas import tpu as pltpu
from jax.sharding import PartitionSpec as P

CAP = 4
ITERS = 3
SLOT_ROWS = 8
EDGE = 128
MESH = pl.DeviceIdType.MESH


def loop(low, high, body):
    if high - low <= 4:
        for k in range(low, high):
            body(k)
    else:
        lax.fori_loop(low, high, lambda k, c: (body(k), c)[1], 0)


def kernel(
    sizes,
    owner_hbm,
    slot_hbm,
    counts_hbm,
    swath_hbm,
    scale_hbm,
    coupling_hbm,
    bg_hbm,
    decay_hbm,
    edge_hbm,
    tiles_hbm,
    values_hbm,
    weights_hbm,
    sol_out,
    res_out,
    owner_s,
    slot_s,
    counts_s,
    swath_s,
    scale_s,
    coupling_s,
    bg,
    decay,
    edge,
    obs_values,
    obs_weights,
    tiles,
    ve,
    hn,
    hs,
    p0,
    p7,
    ew_out,
    ew_in,
    coef,
    diag,
    pe,
    pn,
    ps_,
    weight,
    ask,
    req,
    gather_oh,
    scatter_oh,
    xs,
    xr,
    xp,
    zs,
    zr,
    qp,
    part,
    parts,
    halo_send,
    halo_recv,
    ex_send,
    ex_recv,
    red_send,
    red_recv,
    load_sem,
):
    lon_n, lat_n, fld_n = sizes
    row_n = lat_n * fld_n
    dev_n = lon_n * row_n
    fields, rows, cols = bg.shape
    tile_n, obs_len, patch = tiles.shape
    ext = cols + 2 * EDGE
    per_row = cols // patch
    patch_n = fields * rows * per_row
    pos_n = lon_n * SLOT_ROWS
    bf16, f32 = jnp.bfloat16, jnp.float32

    my_lon = lax.axis_index("lon")
    my_row = lax.axis_index("lat") * fld_n + lax.axis_index("fld")
    me = my_lon * row_n + my_row

    def device(lon, row):
        return {"lon": lon, "lat": row // fld_n, "fld": row % fld_n}

    west, east = (my_lon + lon_n - 1) % lon_n, (my_lon + 1) % lon_n
    north, south = (my_row + row_n - 1) % row_n, (my_row + 1) % row_n
    has_north = (my_row > 0).astype(f32)
    has_south = (my_row < row_n - 1).astype(f32)

    loads = [
        pltpu.make_async_copy(src, dst, load_sem.at[k])
        for k, (src, dst) in enumerate(
            (
                (edge_hbm, edge),
                (bg_hbm, bg),
                (owner_hbm, owner_s),
                (slot_hbm, slot_s),
                (counts_hbm, counts_s),
                (swath_hbm, swath_s),
                (scale_hbm, scale_s),
                (coupling_hbm, coupling_s),
                (values_hbm, obs_values),
                (weights_hbm, obs_weights),
                (decay_hbm, decay),
                (tiles_hbm, tiles),
            )
        )
    ]
    for load in loads:
        load.start()

    barrier = pltpu.get_barrier_semaphore()

    def greet(k):
        other = (me + k) % dev_n
        pl.semaphore_signal(
            barrier, inc=1, device_id=device(other // row_n, other % row_n), device_id_type=MESH
        )

    loop(1, dev_n, greet)

    center = pl.ds(EDGE, cols)
    left, right = pl.ds(0, EDGE), pl.ds(EDGE + cols, EDGE)
    first, final = pl.ds(0, EDGE), pl.ds(cols - EDGE, EDGE)

    def halo_copies(h):
        pairs = (
            (ew_out.at[h, 0], ew_in.at[h, 0], west, my_row),
            (ew_out.at[h, 1], ew_in.at[h, 1], east, my_row),
            (p0.at[h], hs.at[h, :, center], my_lon, north),
            (p7.at[h], hn.at[h, :, center], my_lon, south),
            (p0.at[h, :, first], hs.at[h, :, right], west, north),
            (p0.at[h, :, final], hs.at[h, :, left], east, north),
            (p7.at[h, :, first], hn.at[h, :, right], west, south),
            (p7.at[h, :, final], hn.at[h, :, left], east, south),
        )
        return [
            pltpu.make_async_remote_copy(
                src_ref=src,
                dst_ref=dst,
                send_sem=halo_send.at[h, k],
                recv_sem=halo_recv.at[h, k],
                device_id=device(lon, row),
                device_id_type=MESH,
            )
            for k, (src, dst, lon, row) in enumerate(pairs)
        ]

    lane = lax.broadcasted_iota(jnp.int32, (rows, EDGE), 1)

    def turn(value, by):
        return pltpu.roll(value, by % EDGE, 1) if by % EDGE else value

    def put_fields(h, values):
        to_west = jnp.zeros((rows, EDGE), f32)
        to_east = to_west
        for f, value in enumerate(values):
            ve[h, f, :, EDGE : EDGE + cols] = value
            p0[h, f : f + 1, :] = value[0:1]
            p7[h, f : f + 1, :] = value[rows - 1 : rows]
            to_west = jnp.where(lane == f, turn(value[:, 0:EDGE], f), to_west)
            to_east = jnp.where(lane == f, turn(value[:, cols - EDGE : cols], f + 1), to_east)
        ew_out[h, 0] = to_west
        ew_out[h, 1] = to_east

    def halo_start(h):
        for copy in halo_copies(h):
            copy.start()

    def halo_wait(h):
        for copy in halo_copies(h):
            copy.wait_recv()
        for f in range(fields):
            ve[h, f, :, 0:EDGE] = turn(ew_in[h, 1], EDGE - 1 - f)
            ve[h, f, :, EDGE + cols : ext] = turn(ew_in[h, 0], EDGE - f)

    def swap_start(number, out, into):
        def send(k):
            to = (my_lon + k) % lon_n
            pltpu.make_async_remote_copy(
                src_ref=out.at[to, pl.ds(0, CAP)],
                dst_ref=into.at[my_lon, pl.ds(0, CAP)],
                send_sem=ex_send.at[number],
                recv_sem=ex_recv.at[number],
                device_id=device(to, my_row),
                device_id_type=MESH,
            ).start()

        loop(1, lon_n, send)
        into[my_lon] = out[my_lon]

    def swap_wait(sems, number, buffer):
        some = buffer.at[pl.ds(0, lon_n - 1), pl.ds(0, CAP)]
        pltpu.make_async_copy(some, some, sems.at[number]).wait()

    def total_start(number, value):
        part[number] = value
        parts[number, me] = value

        def send(k):
            other = (me + k) % dev_n
            pltpu.make_async_remote_copy(
                src_ref=part.at[number],
                dst_ref=parts.at[number, me],
                send_sem=red_send.at[number],
                recv_sem=red_recv.at[number],
                device_id=device(other // row_n, other % row_n),
                device_id_type=MESH,
            ).start()

        loop(1, dev_n, send)

    def total_wait(sems, number):
        some = parts.at[number, pl.ds(0, dev_n - 1)]
        pltpu.make_async_copy(some, some, sems.at[number]).wait()

    def total(number):
        total_wait(red_recv, number)
        lanes = jnp.sum(parts[number], axis=0)
        return jnp.sum(lanes, axis=1, keepdims=True)

    def lanes_of(value):
        lane_sum = value[:, 0:128]
        for k in range(1, value.shape[1] // 128):
            lane_sum = lane_sum + value[:, k * 128 : (k + 1) * 128]
        return jnp.sum(lane_sum, axis=0, keepdims=True)

    sub = lax.broadcasted_iota(jnp.int32, (rows, ext), 0)

    def above(value, halo):
        return jnp.where(sub == 0, halo, pltpu.roll(value, 1, 0))

    def below(value, halo):
        return jnp.where(sub == rows - 1, halo, pltpu.roll(value, rows - 1, 0))

    def apply_l(f, value, up_halo, down_halo):
        up, down = above(value, up_halo), below(value, down_halo)
        toward_east = coef[0] * value + coef[1] * up + coef[2] * down
        toward_west = coef[3] * value + coef[4] * up + coef[5] * down
        result = diag[f] * value - coef[6] * up - coef[7] * down
        result = result - pltpu.roll(toward_east, ext - 1, 1) - pltpu.roll(toward_west, 1, 1)
        return result[:, EDGE : EDGE + cols]

    def mixed(first_pass, f):
        acc = coupling_s[f, 0] * first_pass[0]
        for g in range(1, fields):
            acc = acc + coupling_s[f, g] * first_pass[g]
        return acc

    def split3(value):
        high = value.astype(bf16)
        rest = value - high.astype(f32)
        middle = rest.astype(bf16)
        return high, middle, (rest - middle.astype(f32)).astype(bf16)

    row_iota = lax.broadcasted_iota(jnp.int32, (pos_n, 128), 0)
    wide_iota = lax.broadcasted_iota(jnp.int32, (pos_n, patch), 0)
    obs_iota = lax.broadcasted_iota(jnp.int32, (pos_n, obs_len), 1)

    in_use = lax.rem(wide_iota, SLOT_ROWS) < CAP

    loads[0].wait()
    put_fields(1, [edge[e] for e in range(4)])
    loads[1].wait()
    put_fields(0, [bg[f] for f in range(fields)])

    def spread(value, t):
        return jnp.where(wide_iota == positions[t], value, 0.0).astype(bf16)

    def forward(value):
        acc = None
        for t in range(tile_n):
            term = lax.dot_general(
                spread(value, t), tiles[t], (((1,), (1,)), ((), ())), preferred_element_type=f32
            )
            acc = term if acc is None else acc + term
        return acc

    def adjoint(value):
        acc = None
        for t in range(tile_n):
            term = lax.dot_general(
                spread(value, t), tiles[t], (((1,), (0,)), ((), ())), preferred_element_type=f32
            )
            acc = term if acc is None else acc + term
        return acc

    pl.semaphore_wait(barrier, dev_n - 1)
    halo_start(1)
    halo_start(0)

    for load in loads[2:11]:
        load.wait()
    positions = []
    for t in range(tile_n):
        rank = jnp.int32(0)
        for other in range(t):
            rank = rank + (owner_s[other] == owner_s[t]).astype(jnp.int32)
        positions.append(owner_s[t] * SLOT_ROWS + rank)

    asked = jnp.full((pos_n, 128), -1, jnp.int32)
    weight_all = jnp.zeros((pos_n, obs_len), f32)
    values_all = jnp.zeros((pos_n, obs_len), f32)
    for t in range(tile_n):
        number = slot_s[t]
        column, rest = number % per_row, number // per_row
        moved = (column * fields + rest // rows) * rows + rest % rows
        asked = jnp.where(row_iota == positions[t], moved, asked)
        here = wide_iota == positions[t]
        live = here & (obs_iota < counts_s[t])
        weight_all = jnp.where(
            live, obs_weights[t : t + 1, :] * scale_s[swath_s[t]], weight_all
        )
        values_all = jnp.where(here, obs_values[t : t + 1, :], values_all)
    ask[...] = asked.reshape(lon_n, SLOT_ROWS, 128)
    weight[...] = weight_all

    swap_start(0, ask, req)

    loads[11].wait()
    scaled = (weight_all * values_all).astype(bf16).astype(f32)
    zs[0] = adjoint(scaled).reshape(lon_n, SLOT_ROWS, patch)
    swap_start(1, zs.at[0], zr.at[0])

    halo_wait(1)
    w = [ve[1, e] for e in range(4)]
    w_up = [above(w[e], hn[1, e : e + 1, :] * has_north) for e in range(4)]
    w_down = [below(w[e], hs[1, e : e + 1, :] * has_south) for e in range(4)]
    w_west = {e: pltpu.roll(w[e], 1, 1) for e in (0, 2, 3)}
    w_east = {e: pltpu.roll(w[e], ext - 1, 1) for e in (0, 2, 3)}
    e0, e1, e2 = (
        0.5 * (w_west[0] + w[0]),
        0.5 * (w_west[3] + w_up[3]),
        0.5 * (w_west[2] + w_down[2]),
    )
    v0, v1, v2 = (
        0.5 * (w_east[0] + w[0]),
        0.5 * (w_east[2] + w_up[2]),
        0.5 * (w_east[3] + w_down[3]),
    )
    n0, n1 = 0.5 * (w[1] + w_up[1]), 0.5 * (w[1] + w_down[1])
    for k, value in enumerate((e0, e1, e2, v0, v1, v2, n0, n1)):
        coef[k] = value
    degree = n0 + n1 + pltpu.roll(e0 + e1 + e2, ext - 1, 1) + pltpu.roll(v0 + v1 + v2, 1, 1)
    for f in range(fields):
        diag[f] = degree
        diag[f, :, EDGE : EDGE + cols] = decay[f] + degree[:, EDGE : EDGE + cols]

    def up_of(h, f):
        return hn[h, f : f + 1, :] * has_north

    def down_of(h, f):
        return hs[h, f : f + 1, :] * has_south

    halo_wait(0)
    first_pass = [apply_l(f, ve[0, f], up_of(0, f), down_of(0, f)) for f in range(fields)]
    put_fields(2, [mixed(first_pass, f) for f in range(fields)])
    halo_start(2)

    swap_wait(ex_recv, 0, req)
    wanted = req[...].reshape(pos_n, 128)
    wanted = jnp.where(lax.rem(row_iota, SLOT_ROWS) < CAP, wanted, -1)
    wanted = jnp.concatenate([wanted] * (patch_n // 128), axis=1)
    picked = wanted == lax.broadcasted_iota(jnp.int32, (pos_n, patch_n), 1)
    chosen = jnp.where(picked, 1.0, 0.0)
    gather_oh[...] = chosen.astype(bf16)
    if pos_n < 128:
        chosen = jnp.concatenate([chosen, jnp.zeros((128 - pos_n, patch_n), f32)], axis=0)
    scatter_oh[...] = chosen.T.astype(bf16)

    def placed(number):
        arrived = jnp.where(in_use, zr[number].reshape(pos_n, patch), 0.0)
        if pos_n < 128:
            arrived = jnp.concatenate([arrived, jnp.zeros((128 - pos_n, patch), f32)], axis=0)
        high, middle, low = split3(arrived)
        return (
            jnp.dot(scatter_oh[...], low, preferred_element_type=f32)
            + jnp.dot(scatter_oh[...], middle, preferred_element_type=f32)
        ) + jnp.dot(scatter_oh[...], high, preferred_element_type=f32)

    def placed_field(blocks, f):
        return jnp.concatenate(
            [
                blocks[(c * fields + f) * rows : (c * fields + f + 1) * rows]
                for c in range(per_row)
            ],
            axis=1,
        )

    halo_wait(2)
    second = [apply_l(f, ve[2, f], up_of(2, f), down_of(2, f)) for f in range(fields)]
    for f in range(fields):
        qp[f] = second[f]
    swap_wait(ex_recv, 1, zr.at[0])
    blocks = placed(0)
    put_fields(3, [qp[f] + placed_field(blocks, f) for f in range(fields)])
    for f in range(fields):
        sol_out[f] = jnp.zeros((rows, cols), f32)
    pe[...] = jnp.zeros_like(pe)
    pn[...] = jnp.zeros_like(pn)
    ps_[...] = jnp.zeros_like(ps_)
    xp[...] = jnp.zeros_like(xp)

    def iterate(it, norm_before):
        h_r, h_u = 3 + 2 * it, 4 + 2 * it
        squares = jnp.zeros((1, 128), f32)
        for f in range(fields):
            value = ve[h_r, f, :, EDGE : EDGE + cols]
            squares = squares + lanes_of(value * value)
        total_start(2 * it, squares)
        halo_start(h_r)
        stacked = jnp.concatenate(
            [
                ve[h_r, f, :, EDGE + c * patch : EDGE + (c + 1) * patch]
                for c in range(per_row)
                for f in range(fields)
            ],
            axis=0,
        )
        high, middle, low = split3(stacked)
        patches = (
            jnp.dot(gather_oh[...], low, preferred_element_type=f32)
            + jnp.dot(gather_oh[...], middle, preferred_element_type=f32)
        ) + jnp.dot(gather_oh[...], high, preferred_element_type=f32)
        xs[it] = patches.reshape(lon_n, SLOT_ROWS, patch)
        swap_start(2 + 2 * it, xs.at[it], xr.at[it])

        halo_wait(h_r)
        swap_wait(ex_recv, 2 + 2 * it, xr.at[it])
        norm = total(2 * it)
        ratio = norm / norm_before
        for f in range(fields):
            pe[f] = ve[h_r, f] + ratio * pe[f]
        pn[...] = hn[h_r] * has_north + ratio * pn[...]
        ps_[...] = hs[h_r] * has_south + ratio * ps_[...]
        seen = jnp.where(in_use, xr[it].reshape(pos_n, patch), 0.0) + ratio * xp[...]
        xp[...] = seen

        first_pass = [
            apply_l(f, pe[f], pn[f : f + 1, :], ps_[f : f + 1, :]) for f in range(fields)
        ]
        curve = jnp.zeros((1, 128), f32)
        second_in = [mixed(first_pass, f) for f in range(fields)]
        put_fields(h_u, second_in)
        for f in range(fields):
            curve = curve + lanes_of(second_in[f] * first_pass[f])
        halo_start(h_u)

        applied = forward(seen)
        weighted = (weight[...] * applied).astype(bf16).astype(f32)
        curve = curve + lanes_of(applied * weighted)
        total_start(2 * it + 1, curve)
        zs[it + 1] = adjoint(weighted).reshape(lon_n, SLOT_ROWS, patch)
        swap_start(3 + 2 * it, zs.at[it + 1], zr.at[it + 1])

        halo_wait(h_u)
        for f in range(fields):
            qp[f] = apply_l(f, ve[h_u, f], up_of(h_u, f), down_of(h_u, f))
        swap_wait(ex_recv, 3 + 2 * it, zr.at[it + 1])
        blocks = placed(it + 1)
        step = norm / total(2 * it + 1)
        left_over = []
        for f in range(fields):
            sol_out[f] = sol_out[f] + step * pe[f, :, EDGE : EDGE + cols]
            image = qp[f] + placed_field(blocks, f)
            left_over.append(ve[h_r, f, :, EDGE : EDGE + cols] - step * image)
        put_fields(h_r + 2, left_over)
        return norm

    lax.fori_loop(0, ITERS, iterate, jnp.full((1, 1), 1.0, f32))
    for f in range(fields):
        res_out[f] = ve[3 + 2 * ITERS, f, :, EDGE : EDGE + cols]

    def sent_halo(h, carry):
        for copy in halo_copies(h):
            copy.wait_send()
        return carry

    lax.fori_loop(0, 3 + 2 * ITERS, sent_halo, 0)
    swap_wait(ex_send, 0, req)
    swap_wait(ex_send, 1, zr.at[0])

    def sent_rest(it, carry):
        swap_wait(ex_send, 2 + 2 * it, xr.at[it])
        swap_wait(ex_send, 3 + 2 * it, zr.at[it + 1])
        total_wait(red_send, 2 * it)
        total_wait(red_send, 2 * it + 1)
        return carry

    lax.fori_loop(0, ITERS, sent_rest, 0)


def on_device(
    sizes,
    background,
    decay_sq,
    edge_weight,
    coupling,
    obs_tiles,
    obs_values,
    obs_weights,
    obs_counts,
    swath_ids,
    swath_scale,
    tile_owner,
    tile_slot,
):
    fields, rows, cols = background.shape
    tile_n, obs_len, patch = obs_tiles.shape
    lon_n, lat_n, fld_n = sizes
    dev_n = lon_n * lat_n * fld_n
    ext = cols + 2 * EDGE
    pos_n = lon_n * SLOT_ROWS
    patch_n = fields * rows * cols // patch
    halos = 4 + 2 * ITERS
    f32, bf16 = jnp.float32, jnp.bfloat16
    vmem = pl.BlockSpec(memory_space=pltpu.VMEM)
    dma = pltpu.SemaphoreType.DMA
    shape = pltpu.VMEM((fields, rows, cols), f32)
    return pl.pallas_call(
        functools.partial(kernel, sizes),
        out_shape=(shape, shape),
        in_specs=[pl.BlockSpec(memory_space=pltpu.HBM)] * 12,
        out_specs=(vmem, vmem),
        scratch_shapes=[
            pltpu.SMEM(tile_owner.shape, jnp.int32),
            pltpu.SMEM(tile_slot.shape, jnp.int32),
            pltpu.SMEM(obs_counts.shape, jnp.int32),
            pltpu.SMEM(swath_ids.shape, jnp.int32),
            pltpu.SMEM(swath_scale.shape, f32),
            pltpu.SMEM(coupling.shape, f32),
            pltpu.VMEM(background.shape, f32),
            pltpu.VMEM(decay_sq.shape, f32),
            pltpu.VMEM(edge_weight.shape, f32),
            pltpu.VMEM(obs_values.shape, f32),
            pltpu.VMEM(obs_weights.shape, f32),
            pltpu.VMEM((tile_n, obs_len, patch), bf16),
            pltpu.VMEM((halos, fields, rows, ext), f32),
            pltpu.VMEM((halos, fields, ext), f32),
            pltpu.VMEM((halos, fields, ext), f32),
            pltpu.VMEM((halos, fields, cols), f32),
            pltpu.VMEM((halos, fields, cols), f32),
            pltpu.VMEM((halos, 2, rows, EDGE), f32),
            pltpu.VMEM((halos, 2, rows, EDGE), f32),
            pltpu.VMEM((8, rows, ext), f32),
            pltpu.VMEM((fields, rows, ext), f32),
            pltpu.VMEM((fields, rows, ext), f32),
            pltpu.VMEM((fields, ext), f32),
            pltpu.VMEM((fields, ext), f32),
            pltpu.VMEM((pos_n, obs_len), f32),
            pltpu.VMEM((lon_n, SLOT_ROWS, 128), jnp.int32),
            pltpu.VMEM((lon_n, SLOT_ROWS, 128), jnp.int32),
            pltpu.VMEM((pos_n, patch_n), bf16),
            pltpu.VMEM((patch_n, 128), bf16),
            pltpu.VMEM((ITERS, lon_n, SLOT_ROWS, patch), f32),
            pltpu.VMEM((ITERS, lon_n, SLOT_ROWS, patch), f32),
            pltpu.VMEM((pos_n, patch), f32),
            pltpu.VMEM((ITERS + 1, lon_n, SLOT_ROWS, patch), f32),
            pltpu.VMEM((ITERS + 1, lon_n, SLOT_ROWS, patch), f32),
            pltpu.VMEM((fields, rows, cols), f32),
            pltpu.VMEM((2 * ITERS, 1, 128), f32),
            pltpu.VMEM((2 * ITERS, dev_n, 1, 128), f32),
            dma((halos, 8)),
            dma((halos, 8)),
            dma((2 + 2 * ITERS,)),
            dma((2 + 2 * ITERS,)),
            dma((2 * ITERS,)),
            dma((2 * ITERS,)),
            dma((12,)),
        ],
        compiler_params=pltpu.CompilerParams(
            collective_id=0, has_side_effects=True, vmem_limit_bytes=67043328 - 3 * 2**20
        ),
    )(
        tile_owner,
        tile_slot,
        obs_counts,
        swath_ids,
        swath_scale,
        coupling,
        background,
        decay_sq,
        edge_weight,
        obs_tiles,
        obs_values,
        obs_weights,
    )


def solution(mesh):
    sizes = (mesh.shape["lon"], mesh.shape["lat"], mesh.shape["fld"])
    return jax.shard_map(
        functools.partial(on_device, sizes),
        mesh=mesh,
        in_specs=(
            P("group", ("lat", "fld"), "lon"),
            P(None, ("lat", "fld"), "lon"),
            P(None, ("lat", "fld"), "lon"),
            P(),
            P(("lon", "lat", "fld"), None, None),
            P(("group", "lon", "lat", "fld"), None),
            P(("lon", "lat", "fld"), None),
            P(("lon", "lat", "fld")),
            P(("lon", "lat", "fld")),
            P(),
            P(("lon", "lat", "fld")),
            P(("lon", "lat", "fld")),
        ),
        out_specs=(P("group", ("lat", "fld"), "lon"), P("group", ("lat", "fld"), "lon")),
        check_vma=False,
    )
```

```python
import functools

import jax
import jax.numpy as jnp
from jax import lax
from jax.experimental import pallas as pl
from jax.experimental.pallas import tpu as pltpu
from jax.sharding import PartitionSpec as P

CAP = 4
ITERS = 3
SLOT_ROWS = 8
EDGE = 128
MESH = pl.DeviceIdType.MESH


def loop(low, high, body):
    if high - low <= 16:
        for k in range(low, high):
            body(k)
    else:
        lax.fori_loop(low, high, lambda k, c: (body(k), c)[1], 0)


def kernel(
    sizes,
    owner_hbm,
    slot_hbm,
    counts_hbm,
    swath_hbm,
    scale_hbm,
    coupling_hbm,
    bg_hbm,
    decay_hbm,
    edge_hbm,
    tiles_hbm,
    values_hbm,
    weights_hbm,
    sol_out,
    res_out,
    owner_s,
    slot_s,
    counts_s,
    swath_s,
    scale_s,
    coupling_s,
    bg,
    decay,
    edge,
    obs_values,
    obs_weights,
    tiles,
    ve,
    hn,
    hs,
    p0,
    p7,
    ew_out,
    ew_in,
    coef,
    diag,
    pe,
    pn,
    ps_,
    weight,
    ask,
    req,
    gather_oh,
    scatter_oh,
    xs,
    xr,
    xp,
    zs,
    zr,
    qp,
    part,
    parts,
    halo_send,
    halo_recv,
    ex_send,
    ex_recv,
    red_send,
    red_recv,
    load_sem,
):
    lon_n, lat_n, fld_n = sizes
    row_n = lat_n * fld_n
    dev_n = lon_n * row_n
    fields, rows, cols = bg.shape
    tile_n, obs_len, patch = tiles.shape
    ext = cols + 2 * EDGE
    per_row = cols // patch
    patch_n = fields * rows * per_row
    pos_n = lon_n * SLOT_ROWS
    bf16, f32 = jnp.bfloat16, jnp.float32

    my_lon = lax.axis_index("lon")
    my_row = lax.axis_index("lat") * fld_n + lax.axis_index("fld")
    me = my_lon * row_n + my_row

    def device(lon, row):
        return {"lon": lon, "lat": row // fld_n, "fld": row % fld_n}

    west, east = (my_lon + lon_n - 1) % lon_n, (my_lon + 1) % lon_n
    north, south = (my_row + row_n - 1) % row_n, (my_row + 1) % row_n
    has_north = (my_row > 0).astype(f32)
    has_south = (my_row < row_n - 1).astype(f32)

    loads = [
        pltpu.make_async_copy(src, dst, load_sem.at[k])
        for k, (src, dst) in enumerate(
            (
                (edge_hbm, edge),
                (bg_hbm, bg),
                (owner_hbm, owner_s),
                (slot_hbm, slot_s),
                (counts_hbm, counts_s),
                (swath_hbm, swath_s),
                (scale_hbm, scale_s),
                (coupling_hbm, coupling_s),
                (values_hbm, obs_values),
                (weights_hbm, obs_weights),
                (decay_hbm, decay),
                (tiles_hbm, tiles),
            )
        )
    ]
    for load in loads:
        load.start()

    barrier = pltpu.get_barrier_semaphore()

    def greet(k):
        other = (me + k) % dev_n
        pl.semaphore_signal(
            barrier, inc=1, device_id=device(other // row_n, other % row_n), device_id_type=MESH
        )

    loop(1, dev_n, greet)

    center = pl.ds(EDGE, cols)
    left, right = pl.ds(0, EDGE), pl.ds(EDGE + cols, EDGE)
    first, final = pl.ds(0, EDGE), pl.ds(cols - EDGE, EDGE)

    def halo_copies(h):
        pairs = (
            (ew_out.at[h, 0], ew_in.at[h, 0], west, my_row),
            (ew_out.at[h, 1], ew_in.at[h, 1], east, my_row),
            (p0.at[h], hs.at[h, :, center], my_lon, north),
            (p7.at[h], hn.at[h, :, center], my_lon, south),
            (p0.at[h, :, first], hs.at[h, :, right], west, north),
            (p0.at[h, :, final], hs.at[h, :, left], east, north),
            (p7.at[h, :, first], hn.at[h, :, right], west, south),
            (p7.at[h, :, final], hn.at[h, :, left], east, south),
        )
        return [
            pltpu.make_async_remote_copy(
                src_ref=src,
                dst_ref=dst,
                send_sem=halo_send.at[h, k],
                recv_sem=halo_recv.at[h, k],
                device_id=device(lon, row),
                device_id_type=MESH,
            )
            for k, (src, dst, lon, row) in enumerate(pairs)
        ]

    lane = lax.broadcasted_iota(jnp.int32, (rows, EDGE), 1)

    def turn(value, by):
        return pltpu.roll(value, by % EDGE, 1) if by % EDGE else value

    def put_fields(h, values):
        to_west = jnp.zeros((rows, EDGE), f32)
        to_east = to_west
        for f, value in enumerate(values):
            ve[h, f, :, EDGE : EDGE + cols] = value
            p0[h, f : f + 1, :] = value[0:1]
            p7[h, f : f + 1, :] = value[rows - 1 : rows]
            to_west = jnp.where(lane == f, turn(value[:, 0:EDGE], f), to_west)
            to_east = jnp.where(lane == f, turn(value[:, cols - EDGE : cols], f + 1), to_east)
        ew_out[h, 0] = to_west
        ew_out[h, 1] = to_east

    def halo_start(h):
        for copy in halo_copies(h):
            copy.start()

    def halo_wait(h):
        for copy in halo_copies(h):
            copy.wait_recv()
        for f in range(fields):
            ve[h, f, :, 0:EDGE] = turn(ew_in[h, 1], EDGE - 1 - f)
            ve[h, f, :, EDGE + cols : ext] = turn(ew_in[h, 0], EDGE - f)

    def swap_start(number, out, into):
        def send(k):
            to = (my_lon + k) % lon_n
            pltpu.make_async_remote_copy(
                src_ref=out.at[to, pl.ds(0, CAP)],
                dst_ref=into.at[my_lon, pl.ds(0, CAP)],
                send_sem=ex_send.at[number],
                recv_sem=ex_recv.at[number],
                device_id=device(to, my_row),
                device_id_type=MESH,
            ).start()

        loop(1, lon_n, send)
        into[my_lon] = out[my_lon]

    def swap_wait(sems, number, buffer):
        some = buffer.at[pl.ds(0, lon_n - 1), pl.ds(0, CAP)]
        pltpu.make_async_copy(some, some, sems.at[number]).wait()

    def total_start(number, value):
        part[number] = value
        parts[number, me] = value

        def send(k):
            other = (me + k) % dev_n
            pltpu.make_async_remote_copy(
                src_ref=part.at[number],
                dst_ref=parts.at[number, me],
                send_sem=red_send.at[number],
                recv_sem=red_recv.at[number],
                device_id=device(other // row_n, other % row_n),
                device_id_type=MESH,
            ).start()

        loop(1, dev_n, send)

    def total_wait(sems, number):
        some = parts.at[number, pl.ds(0, dev_n - 1)]
        pltpu.make_async_copy(some, some, sems.at[number]).wait()

    def total(number):
        total_wait(red_recv, number)
        lanes = jnp.sum(parts[number], axis=0)
        return jnp.sum(lanes, axis=1, keepdims=True)

    def lanes_of(value):
        lane_sum = value[:, 0:128]
        for k in range(1, value.shape[1] // 128):
            lane_sum = lane_sum + value[:, k * 128 : (k + 1) * 128]
        return jnp.sum(lane_sum, axis=0, keepdims=True)

    sub = lax.broadcasted_iota(jnp.int32, (rows, ext), 0)

    def above(value, halo):
        return jnp.where(sub == 0, halo, pltpu.roll(value, 1, 0))

    def below(value, halo):
        return jnp.where(sub == rows - 1, halo, pltpu.roll(value, rows - 1, 0))

    def apply_l(f, value, up_halo, down_halo):
        up, down = above(value, up_halo), below(value, down_halo)
        toward_east = coef[0] * value + coef[1] * up + coef[2] * down
        toward_west = coef[3] * value + coef[4] * up + coef[5] * down
        result = diag[f] * value - coef[6] * up - coef[7] * down
        result = result - pltpu.roll(toward_east, ext - 1, 1) - pltpu.roll(toward_west, 1, 1)
        return result[:, EDGE : EDGE + cols]

    def mixed(first_pass, f):
        acc = coupling_s[f, 0] * first_pass[0]
        for g in range(1, fields):
            acc = acc + coupling_s[f, g] * first_pass[g]
        return acc

    def split3(value):
        high = value.astype(bf16)
        rest = value - high.astype(f32)
        middle = rest.astype(bf16)
        return high, middle, (rest - middle.astype(f32)).astype(bf16)

    row_iota = lax.broadcasted_iota(jnp.int32, (pos_n, 128), 0)
    wide_iota = lax.broadcasted_iota(jnp.int32, (pos_n, patch), 0)
    obs_iota = lax.broadcasted_iota(jnp.int32, (pos_n, obs_len), 1)

    in_use = lax.rem(wide_iota, SLOT_ROWS) < CAP

    loads[0].wait()
    put_fields(1, [edge[e] for e in range(4)])
    loads[1].wait()
    put_fields(0, [bg[f] for f in range(fields)])

    def spread(value, t):
        return jnp.where(wide_iota == positions[t], value, 0.0).astype(bf16)

    def forward(value):
        acc = None
        for t in range(tile_n):
            term = lax.dot_general(
                spread(value, t), tiles[t], (((1,), (1,)), ((), ())), preferred_element_type=f32
            )
            acc = term if acc is None else acc + term
        return acc

    def adjoint(value):
        acc = None
        for t in range(tile_n):
            term = lax.dot_general(
                spread(value, t), tiles[t], (((1,), (0,)), ((), ())), preferred_element_type=f32
            )
            acc = term if acc is None else acc + term
        return acc

    pl.semaphore_wait(barrier, dev_n - 1)
    halo_start(1)
    halo_start(0)

    for load in loads[2:11]:
        load.wait()
    positions = []
    for t in range(tile_n):
        rank = jnp.int32(0)
        for other in range(t):
            rank = rank + (owner_s[other] == owner_s[t]).astype(jnp.int32)
        positions.append(owner_s[t] * SLOT_ROWS + rank)

    asked = jnp.full((pos_n, 128), -1, jnp.int32)
    weight_all = jnp.zeros((pos_n, obs_len), f32)
    values_all = jnp.zeros((pos_n, obs_len), f32)
    for t in range(tile_n):
        number = slot_s[t]
        column, rest = number % per_row, number // per_row
        moved = (column * fields + rest // rows) * rows + rest % rows
        asked = jnp.where(row_iota == positions[t], moved, asked)
        here = wide_iota == positions[t]
        live = here & (obs_iota < counts_s[t])
        weight_all = jnp.where(
            live, obs_weights[t : t + 1, :] * scale_s[swath_s[t]], weight_all
        )
        values_all = jnp.where(here, obs_values[t : t + 1, :], values_all)
    ask[...] = asked.reshape(lon_n, SLOT_ROWS, 128)
    weight[...] = weight_all

    swap_start(0, ask, req)

    loads[11].wait()
    scaled = (weight_all * values_all).astype(bf16).astype(f32)
    zs[0] = adjoint(scaled).reshape(lon_n, SLOT_ROWS, patch)
    swap_start(1, zs.at[0], zr.at[0])

    halo_wait(1)
    w = [ve[1, e] for e in range(4)]
    w_up = [above(w[e], hn[1, e : e + 1, :] * has_north) for e in range(4)]
    w_down = [below(w[e], hs[1, e : e + 1, :] * has_south) for e in range(4)]
    w_west = {e: pltpu.roll(w[e], 1, 1) for e in (0, 2, 3)}
    w_east = {e: pltpu.roll(w[e], ext - 1, 1) for e in (0, 2, 3)}
    e0, e1, e2 = (
        0.5 * (w_west[0] + w[0]),
        0.5 * (w_west[3] + w_up[3]),
        0.5 * (w_west[2] + w_down[2]),
    )
    v0, v1, v2 = (
        0.5 * (w_east[0] + w[0]),
        0.5 * (w_east[2] + w_up[2]),
        0.5 * (w_east[3] + w_down[3]),
    )
    n0, n1 = 0.5 * (w[1] + w_up[1]), 0.5 * (w[1] + w_down[1])
    for k, value in enumerate((e0, e1, e2, v0, v1, v2, n0, n1)):
        coef[k] = value
    degree = n0 + n1 + pltpu.roll(e0 + e1 + e2, ext - 1, 1) + pltpu.roll(v0 + v1 + v2, 1, 1)
    for f in range(fields):
        diag[f] = degree
        diag[f, :, EDGE : EDGE + cols] = decay[f] + degree[:, EDGE : EDGE + cols]

    def up_of(h, f):
        return hn[h, f : f + 1, :] * has_north

    def down_of(h, f):
        return hs[h, f : f + 1, :] * has_south

    halo_wait(0)
    first_pass = [apply_l(f, ve[0, f], up_of(0, f), down_of(0, f)) for f in range(fields)]
    put_fields(2, [mixed(first_pass, f) for f in range(fields)])
    halo_start(2)

    swap_wait(ex_recv, 0, req)
    wanted = req[...].reshape(pos_n, 128)
    wanted = jnp.where(lax.rem(row_iota, SLOT_ROWS) < CAP, wanted, -1)
    wanted = jnp.concatenate([wanted] * (patch_n // 128), axis=1)
    picked = wanted == lax.broadcasted_iota(jnp.int32, (pos_n, patch_n), 1)
    chosen = jnp.where(picked, 1.0, 0.0)
    gather_oh[...] = chosen.astype(bf16)
    if pos_n < 128:
        chosen = jnp.concatenate([chosen, jnp.zeros((128 - pos_n, patch_n), f32)], axis=0)
    scatter_oh[...] = chosen.T.astype(bf16)

    def placed(number):
        arrived = jnp.where(in_use, zr[number].reshape(pos_n, patch), 0.0)
        if pos_n < 128:
            arrived = jnp.concatenate([arrived, jnp.zeros((128 - pos_n, patch), f32)], axis=0)
        high, middle, low = split3(arrived)
        return (
            jnp.dot(scatter_oh[...], low, preferred_element_type=f32)
            + jnp.dot(scatter_oh[...], middle, preferred_element_type=f32)
        ) + jnp.dot(scatter_oh[...], high, preferred_element_type=f32)

    def placed_field(blocks, f):
        return jnp.concatenate(
            [
                blocks[(c * fields + f) * rows : (c * fields + f + 1) * rows]
                for c in range(per_row)
            ],
            axis=1,
        )

    halo_wait(2)
    second = [apply_l(f, ve[2, f], up_of(2, f), down_of(2, f)) for f in range(fields)]
    for f in range(fields):
        qp[f] = second[f]
    swap_wait(ex_recv, 1, zr.at[0])
    blocks = placed(0)
    put_fields(3, [qp[f] + placed_field(blocks, f) for f in range(fields)])
    for f in range(fields):
        sol_out[f] = jnp.zeros((rows, cols), f32)
    pe[...] = jnp.zeros_like(pe)
    pn[...] = jnp.zeros_like(pn)
    ps_[...] = jnp.zeros_like(ps_)
    xp[...] = jnp.zeros_like(xp)

    def iterate(it, norm_before):
        h_r, h_u = 3 + 2 * it, 4 + 2 * it
        squares = jnp.zeros((1, 128), f32)
        for f in range(fields):
            value = ve[h_r, f, :, EDGE : EDGE + cols]
            squares = squares + lanes_of(value * value)
        total_start(2 * it, squares)
        halo_start(h_r)
        stacked = jnp.concatenate(
            [
                ve[h_r, f, :, EDGE + c * patch : EDGE + (c + 1) * patch]
                for c in range(per_row)
                for f in range(fields)
            ],
            axis=0,
        )
        high, middle, low = split3(stacked)
        patches = (
            jnp.dot(gather_oh[...], low, preferred_element_type=f32)
            + jnp.dot(gather_oh[...], middle, preferred_element_type=f32)
        ) + jnp.dot(gather_oh[...], high, preferred_element_type=f32)
        xs[it] = patches.reshape(lon_n, SLOT_ROWS, patch)
        swap_start(2 + 2 * it, xs.at[it], xr.at[it])

        halo_wait(h_r)
        swap_wait(ex_recv, 2 + 2 * it, xr.at[it])
        norm = total(2 * it)
        ratio = norm / norm_before
        for f in range(fields):
            pe[f] = ve[h_r, f] + ratio * pe[f]
        pn[...] = hn[h_r] * has_north + ratio * pn[...]
        ps_[...] = hs[h_r] * has_south + ratio * ps_[...]
        seen = jnp.where(in_use, xr[it].reshape(pos_n, patch), 0.0) + ratio * xp[...]
        xp[...] = seen

        first_pass = [
            apply_l(f, pe[f], pn[f : f + 1, :], ps_[f : f + 1, :]) for f in range(fields)
        ]
        curve = jnp.zeros((1, 128), f32)
        second_in = [mixed(first_pass, f) for f in range(fields)]
        put_fields(h_u, second_in)
        for f in range(fields):
            curve = curve + lanes_of(second_in[f] * first_pass[f])
        halo_start(h_u)

        applied = forward(seen)
        weighted = (weight[...] * applied).astype(bf16).astype(f32)
        curve = curve + lanes_of(applied * weighted)
        total_start(2 * it + 1, curve)
        zs[it + 1] = adjoint(weighted).reshape(lon_n, SLOT_ROWS, patch)
        swap_start(3 + 2 * it, zs.at[it + 1], zr.at[it + 1])

        halo_wait(h_u)
        for f in range(fields):
            qp[f] = apply_l(f, ve[h_u, f], up_of(h_u, f), down_of(h_u, f))
        swap_wait(ex_recv, 3 + 2 * it, zr.at[it + 1])
        blocks = placed(it + 1)
        step = norm / total(2 * it + 1)
        left_over = []
        for f in range(fields):
            sol_out[f] = sol_out[f] + step * pe[f, :, EDGE : EDGE + cols]
            image = qp[f] + placed_field(blocks, f)
            left_over.append(ve[h_r, f, :, EDGE : EDGE + cols] - step * image)
        put_fields(h_r + 2, left_over)
        return norm

    lax.fori_loop(0, ITERS, iterate, jnp.full((1, 1), 1.0, f32))
    for f in range(fields):
        res_out[f] = ve[3 + 2 * ITERS, f, :, EDGE : EDGE + cols]

    def sent_halo(h, carry):
        for copy in halo_copies(h):
            copy.wait_send()
        return carry

    lax.fori_loop(0, 3 + 2 * ITERS, sent_halo, 0)
    swap_wait(ex_send, 0, req)
    swap_wait(ex_send, 1, zr.at[0])

    def sent_rest(it, carry):
        swap_wait(ex_send, 2 + 2 * it, xr.at[it])
        swap_wait(ex_send, 3 + 2 * it, zr.at[it + 1])
        total_wait(red_send, 2 * it)
        total_wait(red_send, 2 * it + 1)
        return carry

    lax.fori_loop(0, ITERS, sent_rest, 0)


def on_device(
    sizes,
    background,
    decay_sq,
    edge_weight,
    coupling,
    obs_tiles,
    obs_values,
    obs_weights,
    obs_counts,
    swath_ids,
    swath_scale,
    tile_owner,
    tile_slot,
):
    fields, rows, cols = background.shape
    tile_n, obs_len, patch = obs_tiles.shape
    lon_n, lat_n, fld_n = sizes
    dev_n = lon_n * lat_n * fld_n
    ext = cols + 2 * EDGE
    pos_n = lon_n * SLOT_ROWS
    patch_n = fields * rows * cols // patch
    halos = 4 + 2 * ITERS
    f32, bf16 = jnp.float32, jnp.bfloat16
    vmem = pl.BlockSpec(memory_space=pltpu.VMEM)
    dma = pltpu.SemaphoreType.DMA
    shape = pltpu.VMEM((fields, rows, cols), f32)
    return pl.pallas_call(
        functools.partial(kernel, sizes),
        out_shape=(shape, shape),
        in_specs=[pl.BlockSpec(memory_space=pltpu.HBM)] * 12,
        out_specs=(vmem, vmem),
        scratch_shapes=[
            pltpu.SMEM(tile_owner.shape, jnp.int32),
            pltpu.SMEM(tile_slot.shape, jnp.int32),
            pltpu.SMEM(obs_counts.shape, jnp.int32),
            pltpu.SMEM(swath_ids.shape, jnp.int32),
            pltpu.SMEM(swath_scale.shape, f32),
            pltpu.SMEM(coupling.shape, f32),
            pltpu.VMEM(background.shape, f32),
            pltpu.VMEM(decay_sq.shape, f32),
            pltpu.VMEM(edge_weight.shape, f32),
            pltpu.VMEM(obs_values.shape, f32),
            pltpu.VMEM(obs_weights.shape, f32),
            pltpu.VMEM((tile_n, obs_len, patch), bf16),
            pltpu.VMEM((halos, fields, rows, ext), f32),
            pltpu.VMEM((halos, fields, ext), f32),
            pltpu.VMEM((halos, fields, ext), f32),
            pltpu.VMEM((halos, fields, cols), f32),
            pltpu.VMEM((halos, fields, cols), f32),
            pltpu.VMEM((halos, 2, rows, EDGE), f32),
            pltpu.VMEM((halos, 2, rows, EDGE), f32),
            pltpu.VMEM((8, rows, ext), f32),
            pltpu.VMEM((fields, rows, ext), f32),
            pltpu.VMEM((fields, rows, ext), f32),
            pltpu.VMEM((fields, ext), f32),
            pltpu.VMEM((fields, ext), f32),
            pltpu.VMEM((pos_n, obs_len), f32),
            pltpu.VMEM((lon_n, SLOT_ROWS, 128), jnp.int32),
            pltpu.VMEM((lon_n, SLOT_ROWS, 128), jnp.int32),
            pltpu.VMEM((pos_n, patch_n), bf16),
            pltpu.VMEM((patch_n, 128), bf16),
            pltpu.VMEM((ITERS, lon_n, SLOT_ROWS, patch), f32),
            pltpu.VMEM((ITERS, lon_n, SLOT_ROWS, patch), f32),
            pltpu.VMEM((pos_n, patch), f32),
            pltpu.VMEM((ITERS + 1, lon_n, SLOT_ROWS, patch), f32),
            pltpu.VMEM((ITERS + 1, lon_n, SLOT_ROWS, patch), f32),
            pltpu.VMEM((fields, rows, cols), f32),
            pltpu.VMEM((2 * ITERS, 1, 128), f32),
            pltpu.VMEM((2 * ITERS, dev_n, 1, 128), f32),
            dma((halos, 8)),
            dma((halos, 8)),
            dma((2 + 2 * ITERS,)),
            dma((2 + 2 * ITERS,)),
            dma((2 * ITERS,)),
            dma((2 * ITERS,)),
            dma((12,)),
        ],
        compiler_params=pltpu.CompilerParams(
            collective_id=0, has_side_effects=True, vmem_limit_bytes=67043328 - 3 * 2**20
        ),
    )(
        tile_owner,
        tile_slot,
        obs_counts,
        swath_ids,
        swath_scale,
        coupling,
        background,
        decay_sq,
        edge_weight,
        obs_tiles,
        obs_values,
        obs_weights,
    )


def solution(mesh):
    sizes = (mesh.shape["lon"], mesh.shape["lat"], mesh.shape["fld"])
    return jax.shard_map(
        functools.partial(on_device, sizes),
        mesh=mesh,
        in_specs=(
            P("group", ("lat", "fld"), "lon"),
            P(None, ("lat", "fld"), "lon"),
            P(None, ("lat", "fld"), "lon"),
            P(),
            P(("lon", "lat", "fld"), None, None),
            P(("group", "lon", "lat", "fld"), None),
            P(("lon", "lat", "fld"), None),
            P(("lon", "lat", "fld")),
            P(("lon", "lat", "fld")),
            P(),
            P(("lon", "lat", "fld")),
            P(("lon", "lat", "fld")),
        ),
        out_specs=(P("group", ("lat", "fld"), "lon"), P("group", ("lat", "fld"), "lon")),
        check_vma=False,
    )
```
